128 devices in a mesh: front: 8 (over x, core), grp: 16 (over z, y).
Axes of the slice: x: 4, y: 4, z: 4, core: 2. Of those that a mesh axis runs over, the one named last changes fastest.
Arguments:
- front_in: bfloat16 [8, 8192, 8192], P('front', None, 'grp'), may hold values from -6 to 6
- panel_inverse: float32 [8, 2, 256, 256], P('front'), may hold values from -2 to 2, as said below
- tile_mask: int32 [8, 32, 32], P('front', None, 'grp'), may hold values 0 or 1
- tile_map: int32 [8, 16, 8], P('front', 'grp'), may hold values from 0 to 1023, as said below
Outputs:
- front_out: bfloat16 [8, 8192, 8192], P('front', None, 'grp')
- parent_tiles: float32 [1024, 256, 256], P(('front', 'grp'))
The draws below stay inside these ranges and needn't reach their ends.
Inputs may be any that keep to these rules, and one draw needn't show every extreme that they name: `panel_inverse`: lower triangular, with a positive diagonal. `tile_map`: entry s names device s // 8 of the mesh (front slowest), parent front s // 128. The 8 tiles of one front and one index of grp go to exactly 2 tiles each of 4 distinct parent fronts. Of all tiles from fronts' devices with the same grp index that go to one parent front, no two go to the same device of that parent's group.
All inputs are finite; a program needn't handle non-finite values. No bound on the sum of `tile_mask` on one device may be relied on, other than what follows from the above.
Results may differ from the reference program's by a relative error of at most 0.006.
Values may be sent and summed in bfloat16 or wider, within the bound.
A program may use at most 192 MiB of HBM per device.

```python
import math
import jax
import jax.numpy as jnp
from jax import lax

TILE = 256
ORDER = 8192
FRONTS = 8
TILES = 32
COLS_DEV = 2
CONTRIB = 8
ROWS_OUT = 4
PER_PARENT = 2
SLOTS = 8
N_GRP = 16


def draw_panel_inverse(key, part):
    first_key, second_key = jax.random.split(jax.random.fold_in(key, 11))
    shape = (FRONTS, 2, TILE, TILE)
    lower_part = jax.random.normal(first_key, shape, jnp.float32) * (0.25 / math.sqrt(TILE))
    diagonal = jax.random.uniform(second_key, shape[:-1], jnp.float32, 0.15, 0.45)
    rows = jax.lax.broadcasted_iota(jnp.int32, (TILE, TILE), 0)
    cols = jax.lax.broadcasted_iota(jnp.int32, (TILE, TILE), 1)
    result = jnp.where(rows > cols, lower_part, 0.0) + jnp.where(rows == cols, diagonal[..., None], 0.0)
    return result.astype(jnp.float32)


def draw_tile_map(key, part):
    front_key, owner_key, slot_key = jax.random.split(jax.random.fold_in(key, 23), 3)
    front_keys = jax.random.split(front_key, FRONTS * N_GRP)
    front_perm = jax.vmap(lambda single: jax.random.permutation(single, FRONTS))(front_keys)
    front_perm = front_perm.reshape(FRONTS, N_GRP, FRONTS).astype(jnp.int32)
    owner_keys = jax.random.split(owner_key, FRONTS * N_GRP)
    owner_perm = jax.vmap(lambda single: jax.random.permutation(single, N_GRP))(owner_keys)
    owner_perm = owner_perm.reshape(FRONTS, N_GRP, N_GRP).astype(jnp.int32)
    number = jnp.arange(CONTRIB, dtype=jnp.int32)
    parent = front_perm[:, :, number // PER_PARENT]
    within = (number % PER_PARENT)[None, None, :]
    source = jnp.arange(FRONTS, dtype=jnp.int32)[:, None, None]
    column = jnp.arange(N_GRP, dtype=jnp.int32)[None, :, None]
    position = source * PER_PARENT + within
    owner = owner_perm[parent, column, position]
    slot = jax.random.randint(slot_key, (FRONTS, N_GRP, CONTRIB), 0, SLOTS, jnp.int32)
    return ((parent * N_GRP + owner) * SLOTS + slot).astype(jnp.int32)


def place_ends(entries, own_key, low, high):
    longest = entries.shape.index(max(entries.shape))
    spots = []
    for shift in (0, 1):
        where = [jax.random.randint(jax.random.fold_in(own_key, axis), (), 0, length) for axis, length in enumerate(entries.shape)]
        where[longest] = (where[longest] + shift) % entries.shape[longest]
        spots.append(tuple(where))
    return entries.at[spots[0]].set(low).at[spots[1]].set(high)


def steps_of(key, dims, cuts, low, top_value):
    gain, own = 1.0, jax.random.fold_in(key, 6)
    for dim, parts in cuts:
        heights = jnp.exp(jax.random.uniform(jax.random.fold_in(own, dim), (parts,), jnp.float32, low / len(cuts), top_value / len(cuts)))
        gain = gain * jnp.repeat(heights, dims[dim] // parts).reshape([-1 if axis == dim else 1 for axis in range(len(dims))])
    return gain


def scatter_about(rng, extent, deviation, bound, shards=(), kind=jnp.bfloat16):
    values = deviation * jax.random.normal(rng, extent, jnp.float32)
    if shards:
        values = values * steps_of(rng, extent, shards, -0.22, 0.18)
    return jnp.clip(values, -bound, bound).astype(kind)


def setup_inputs(seed: int = 0) -> dict:
    splits = jax.random.split(jax.random.key(seed), 5)
    return {
        "front_in": scatter_about(splits[0], (FRONTS, ORDER, ORDER), 1.0, 6.0, ((0, 8), (2, 16))),
        "panel_inverse": draw_panel_inverse(jax.random.fold_in(splits[4], 71), 0),
        "tile_mask": place_ends((jax.random.randint(splits[2], (FRONTS, TILES, TILES), 0, 4) < 3).astype(jnp.int32), jax.random.fold_in(splits[2], 1), 0, 1),
        "tile_map": draw_tile_map(jax.random.fold_in(splits[4], 71), 0),
    }


def one_front(items):
    front, inverse, mask = items
    working = front.astype(jnp.float32)
    row_tiles = (jnp.arange(ORDER, dtype=jnp.int32) // TILE)[:, None]
    tile_index = jnp.arange(TILES, dtype=jnp.int32)
    keep_mask = mask.astype(jnp.float32)

    def factor(block, which):
        product = jnp.dot(block, inverse[which].T, precision=lax.Precision.HIGHEST, preferred_element_type=jnp.float32)
        return jnp.where(row_tiles > which, product, 0.0).astype(jnp.bfloat16)

    def trailing(working, panel, which):
        update = jnp.dot(panel, panel.T, preferred_element_type=jnp.float32)
        inside = (tile_index[:, None] > which) & (tile_index[None, :] > which)
        keep = keep_mask * inside.astype(jnp.float32)
        update = update.reshape(TILES, TILE, TILES, TILE) * keep[:, None, :, None]
        return working - update.reshape(ORDER, ORDER)

    first = factor(working[:, :TILE], 0)
    working = trailing(working, first, 0)
    second = factor(working[:, TILE:2 * TILE], 1)
    working = trailing(working, second, 1)
    result = working.astype(jnp.bfloat16)
    result = result.at[:, :TILE].set(jnp.where(row_tiles > 0, first, result[:, :TILE]))
    result = result.at[:, TILE:2 * TILE].set(jnp.where(row_tiles > 1, second, result[:, TILE:2 * TILE]))
    return result


def reference(front_in, panel_inverse, tile_mask, tile_map):
    front_out = lax.map(one_front, (front_in, panel_inverse, tile_mask))
    bottom = front_out[:, (TILES - ROWS_OUT) * TILE:, :]
    bottom = bottom.reshape(FRONTS, ROWS_OUT, TILE, N_GRP, COLS_DEV, TILE)
    bottom = jnp.transpose(bottom, (0, 3, 4, 1, 2, 5)).reshape(FRONTS * N_GRP * CONTRIB, TILE, TILE)
    parent_tiles = jax.ops.segment_sum(bottom.astype(jnp.float32), tile_map.reshape(-1), num_segments=FRONTS * N_GRP * SLOTS)
    return front_out, parent_tiles
```

```python
import functools

import jax
import jax.numpy as jnp
from jax import lax
from jax.experimental import pallas as pl
from jax.experimental.pallas import tpu as pltpu
from jax.sharding import PartitionSpec as P

TILE = 256
TILES = 32
ORDER = TILE * TILES
WIDTH = 2 * TILE
FRONTS = 8
GROUP = 16
SLOTS = 8
ROWS_OUT = 4
CHUNK = 32
SUB = TILE // (4 * CHUNK)
STEPS = (TILES - 1) * SUB
LAG = 3
DEPTH = 7
MESH = pl.DeviceIdType.MESH


def order_row(position):
    return jnp.where(position == 0, 1, jnp.where(position <= ROWS_OUT, 27 + position, TILES - position))


def tree_place(tree, y, z):
    a = (y, z, lax.rem(4 - y, 4), lax.rem(4 - z, 4))[tree]
    b = (z, lax.rem(4 - y, 4), lax.rem(4 - z, 4), y)[tree]
    depth = jnp.where((a == 0) & (b > 0), b + 4, a + b)
    send_a = ((b == 0) & (a < 3)) | ((b > 0) & (a == 3))
    send_b = (a > 0) & (b < 3)
    return depth, send_a, send_b


def dot_t(x, y):
    return lax.dot_general(x, y, (((1,), (1,)), ((), ())), preferred_element_type=jnp.float32)


def dot_n(x, y):
    return lax.dot_general(x, y, (((1,), (0,)), ((), ())), preferred_element_type=jnp.float32)


def panels_kernel(
    front, inverse, mask_rows, out, contrib,
    own, cols, panel, inv_parts, first_one, mask_one, own_t,
    recv_sem, mask_recv, send_sem, mask_send, own_sem, out_sem,
):
    g = lax.axis_index("grp")
    y, z = lax.rem(g, 4), g // 4
    is_root = g == 0

    def at(yy, zz):
        return {"grp": lax.rem(zz + 4, 4) * 4 + lax.rem(yy + 4, 4)}

    hop = (at(y + 1, z), at(y, z + 1), at(y - 1, z), at(y, z - 1))
    places = [tree_place(k, y, z) for k in range(4)]
    last_depth = functools.reduce(jnp.maximum, [p[0] for p in places])

    def rows_of(k, c):
        base = order_row(c // SUB) * TILE + k * (TILE // 4) + lax.rem(c, SUB) * CHUNK
        return pl.ds(pl.multiple_of(base, CHUNK), CHUNK)

    def mask_part(k):
        return pl.ds(k * 8, 8)

    barrier = pltpu.get_barrier_semaphore()
    for target in hop:
        pl.semaphore_signal(barrier, inc=1, device_id=target, device_id_type=MESH)

    @pl.when(is_root)
    def _():
        for k in range(4):
            pltpu.make_async_copy(
                mask_rows.at[mask_part(k), pl.ds(TILE, TILE)], mask_one.at[mask_part(k)], mask_recv.at[k]
            ).start()

        def load(c, carry):
            for k in range(4):
                pltpu.make_async_copy(front.at[0, rows_of(k, c)], cols.at[rows_of(k, c)], recv_sem.at[k, c]).start()
            return carry

        lax.fori_loop(0, STEPS, load, 0)

    for i in range(8):
        rows = pl.ds(i * 1024, 1024)
        pltpu.make_async_copy(front.at[0, rows], own.at[rows], own_sem.at[i]).start()

    for which in range(2):
        flipped = inverse[0, which].T
        high = flipped.astype(jnp.bfloat16)
        inv_parts[2 * which] = high
        inv_parts[2 * which + 1] = (flipped - high.astype(jnp.float32)).astype(jnp.bfloat16)
    panel[pl.ds(0, TILE), :] = jnp.zeros((TILE, WIDTH), jnp.bfloat16)

    pl.semaphore_wait(barrier, 4)

    def forward(k, source, send, recv):
        _, send_a, send_b = places[k]
        for side, go, target in ((0, send_a, hop[k]), (1, send_b, hop[(k + 1) % 4])):
            @pl.when(go)
            def _():
                pltpu.make_async_remote_copy(
                    src_ref=source, dst_ref=source, send_sem=send.at[k, side], recv_sem=recv,
                    device_id=target, device_id_type=MESH,
                ).start()

    def step(t, carry):
        for k in range(4):
            c = t - LAG * places[k][0]

            @pl.when(c == 0)
            def _():
                part = mask_one.at[mask_part(k)]
                pltpu.make_async_copy(part, part, mask_recv.at[k]).wait()
                forward(k, part, mask_send, mask_recv.at[k])

            @pl.when((c >= 0) & (c < STEPS))
            def _():
                part = cols.at[rows_of(k, c)]
                pltpu.make_async_copy(part, part, recv_sem.at[k, c]).wait()
                forward(k, part, send_sem, recv_sem.at[k, c])

        done = t - LAG * last_depth

        @pl.when((done >= 0) & (done < STEPS) & (lax.rem(done + 1, SUB) == 0))
        def _():
            position = done // SUB
            r = order_row(position)
            rows = pl.ds(pl.multiple_of(r * TILE, TILE), TILE)
            left = cols[rows, pl.ds(0, TILE)]
            first = (dot_n(left, inv_parts[0]) + dot_n(left, inv_parts[1])).astype(jnp.bfloat16)
            panel[rows, pl.ds(0, TILE)] = first

            @pl.when(position == 0)
            def _():
                first_one[...] = first
                panel[rows, pl.ds(TILE, TILE)] = jnp.zeros((TILE, TILE), jnp.bfloat16)

            @pl.when(position > 0)
            def _():
                right = cols[rows, pl.ds(TILE, TILE)].astype(jnp.float32)
                right = right - dot_t(first, first_one[...]) * mask_one[pl.ds(r, 1), :]
                high = right.astype(jnp.bfloat16)
                low = (right - high.astype(jnp.float32)).astype(jnp.bfloat16)
                second = dot_n(high, inv_parts[2]) + dot_n(high, inv_parts[3]) + dot_n(low, inv_parts[2])
                panel[rows, pl.ds(TILE, TILE)] = second.astype(jnp.bfloat16)

        return carry

    lax.fori_loop(0, STEPS + LAG * DEPTH, step, 0)

    own_t[...] = panel[pl.ds(pl.multiple_of(g * WIDTH, WIDTH), WIDTH), :].T

    for i in range(8):
        rows = pl.ds(i * 1024, 1024)
        pltpu.make_async_copy(front.at[0, rows], own.at[rows], own_sem.at[i]).wait()

    def update(i, carry):
        rows = pl.ds(pl.multiple_of(i * 512, 512), 512)
        product = dot_n(panel[rows, :], own_t[...])
        for h in range(2):
            r = 2 * i + h
            part = pl.ds(pl.multiple_of(r * TILE, TILE), TILE)
            value = own[part, :].astype(jnp.float32) - product[h * TILE:(h + 1) * TILE] * mask_rows[pl.ds(r, 1), :]
            value = value.astype(jnp.bfloat16)
            lane = lax.broadcasted_iota(jnp.int32, (TILE, WIDTH), 1) // TILE
            final = is_root & (r > lane)
            own[part, :] = jnp.where(final, panel[part, :], value)
        pltpu.make_async_copy(own.at[rows], out.at[0, rows], out_sem.at[i]).start()
        return carry

    lax.fori_loop(0, 16, update, 0)

    for k in range(4):
        _, send_a, send_b = places[k]
        for side, go in ((0, send_a), (1, send_b)):
            @pl.when(go)
            def _():
                part = mask_one.at[mask_part(k)]
                pltpu.make_async_copy(part, part, mask_send.at[k, side]).wait()
                sent = cols.at[pl.ds(0, STEPS * CHUNK)]
                pltpu.make_async_copy(sent, sent, send_sem.at[k, side]).wait()

    for c in range(2):
        for r in range(ROWS_OUT):
            contrib[c * ROWS_OUT + r] = own[pl.ds((28 + r) * TILE, TILE), pl.ds(c * TILE, TILE)]

    for i in range(16):
        rows = pl.ds(i * 512, 512)
        pltpu.make_async_copy(own.at[rows], out.at[0, rows], out_sem.at[i]).wait()


def panels(front, inverse, mask_rows):
    vmem = pl.BlockSpec(memory_space=pltpu.VMEM)
    anywhere = pl.BlockSpec(memory_space=pl.ANY)
    return pl.pallas_call(
        panels_kernel,
        out_shape=(
            jax.ShapeDtypeStruct((1, ORDER, WIDTH), jnp.bfloat16),
            jax.ShapeDtypeStruct((SLOTS, TILE, TILE), jnp.bfloat16),
        ),
        in_specs=[anywhere, vmem, vmem],
        out_specs=(anywhere, vmem),
        scratch_shapes=[
            pltpu.VMEM((ORDER, WIDTH), jnp.bfloat16),
            pltpu.VMEM((ORDER, WIDTH), jnp.bfloat16),
            pltpu.VMEM((ORDER, WIDTH), jnp.bfloat16),
            pltpu.VMEM((4, TILE, TILE), jnp.bfloat16),
            pltpu.VMEM((TILE, TILE), jnp.bfloat16),
            pltpu.VMEM((TILES, TILE), jnp.float32),
            pltpu.VMEM((WIDTH, WIDTH), jnp.bfloat16),
            pltpu.SemaphoreType.DMA((4, STEPS)),
            pltpu.SemaphoreType.DMA((4,)),
            pltpu.SemaphoreType.DMA((4, 2)),
            pltpu.SemaphoreType.DMA((4, 2)),
            pltpu.SemaphoreType.DMA((8,)),
            pltpu.SemaphoreType.DMA((16,)),
        ],
        compiler_params=pltpu.CompilerParams(
            collective_id=0, has_side_effects=True, vmem_limit_bytes=64 * 1024 * 1024 - 65536
        ),
        name="panels",
    )(front, inverse, mask_rows)


def place(destination, labels, values, count):
    selector = (destination[None, :] == jnp.arange(count, dtype=jnp.int32)[:, None]) & (labels >= 0)[None, :]
    tiles = jnp.einsum("dt,tab->dab", selector.astype(jnp.bfloat16), values, preferred_element_type=jnp.float32)
    marks = jnp.max(jnp.where(selector, labels[None, :], -1), axis=1)
    return tiles.astype(jnp.bfloat16), marks[:, None]


def shards(front_in, panel_inverse, tile_mask, tile_map):
    mask_rows = jnp.repeat(tile_mask[0].astype(jnp.float32), TILE, axis=1)
    result, tiles = panels(front_in, panel_inverse, mask_rows)

    labels = tile_map[0, 0]
    parent = labels // (GROUP * SLOTS)
    number = jnp.arange(SLOTS, dtype=jnp.int32)
    earlier = (parent[None, :] == parent[:, None]) & (number[None, :] < number[:, None])
    rank = jnp.sum(earlier.astype(jnp.int32), axis=1)
    tiles, marks = place(parent * 2 + rank, labels, tiles, 2 * FRONTS)
    tiles = lax.all_to_all(tiles, "front", split_axis=0, concat_axis=0, tiled=True)
    marks = lax.all_to_all(marks, "front", split_axis=0, concat_axis=0, tiled=True)[:, 0]
    tiles, marks = place(marks // SLOTS % GROUP, marks, tiles, GROUP)
    tiles = lax.all_to_all(tiles, "grp", split_axis=0, concat_axis=0, tiled=True)
    marks = lax.all_to_all(marks, "grp", split_axis=0, concat_axis=0, tiled=True)[:, 0]
    picker = (marks[None, :] % SLOTS == number[:, None]) & (marks >= 0)[None, :]
    parent_tiles = jnp.einsum("sk,kab->sab", picker.astype(jnp.bfloat16), tiles, preferred_element_type=jnp.float32)
    return result, parent_tiles


def solution(mesh):
    in_specs = (
        P("front", None, "grp"),
        P("front", None, None, None),
        P("front", None, "grp"),
        P("front", "grp", None),
    )
    out_specs = (P("front", None, "grp"), P(("front", "grp"), None, None))
    return jax.shard_map(shards, mesh=mesh, in_specs=in_specs, out_specs=out_specs, check_vma=False)
```

```python
import jax
import jax.numpy as jnp
from jax import lax
from jax.experimental import pallas as pl
from jax.experimental.pallas import tpu as pltpu
from jax.sharding import PartitionSpec as P

TILE = 256
TILES = 32
ORDER = TILE * TILES
WIDTH = 2 * TILE
FRONTS = 8
GROUP = 16
SLOTS = 8
ROWS_OUT = 4
CHUNK = 32
SUB = TILE // (4 * CHUNK)
SHIFT = SUB.bit_length() - 1
STEPS = (TILES - 1) * SUB
LAG = 5
DEPTH = 5
PIECES = 10
BLOCK = 512
MESH = pl.DeviceIdType.MESH

TREE_DEPTH = (0, 1, 2, 3, 3, 2, 3, 4, 4, 3, 4, 5, 3, 2, 3, 4)
TREE_SERVES = ((0,), (0, 1, 3), (0, 3), (), (), (0, 1, 2), (0,), (), (), (0, 2), (0,), (), (), (2,), (0,), ())


def entry(table, place):
    words = []
    for half in (table[:8], table[8:]):
        word = sum(value << (4 * i) for i, value in enumerate(half))
        words.append(word - (1 << 32) if word >= 1 << 31 else word)
    word = jnp.where(place < 8, words[0], words[1])
    return lax.shift_right_logical(word, lax.rem(place, 8) * 4) & 15


def tree_place(tree, y, z):
    a = (y, z, lax.rem(4 - y, 4), lax.rem(4 - z, 4))[tree]
    b = (z, lax.rem(4 - y, 4), lax.rem(4 - z, 4), y)[tree]
    place = b * 4 + a
    count = entry([len(v) for v in TREE_SERVES], place)
    turns = [entry([v[i] if len(v) > i else 0 for v in TREE_SERVES], place) for i in range(3)]
    return entry(TREE_DEPTH, place), count, [(turn + tree) & 3 for turn in turns]


def order_row(position):
    return jnp.where(position == 0, 1, jnp.where(position <= ROWS_OUT, 27 + position, TILES - position))


def dot_t(x, y):
    return lax.dot_general(x, y, (((1,), (1,)), ((), ())), preferred_element_type=jnp.float32)


def dot_n(x, y):
    return lax.dot_general(x, y, (((1,), (0,)), ((), ())), preferred_element_type=jnp.float32)


def wait_for(ref, sem):
    pltpu.make_async_copy(ref, ref, sem).wait()


def send(source, target, send_sem, recv_sem, device):
    pltpu.make_async_remote_copy(
        src_ref=source, dst_ref=target, send_sem=send_sem, recv_sem=recv_sem, device_id=device, device_id_type=MESH
    ).start()


def fronts_kernel(
    front, inverse, mask, labels, out, arrived, arrived_marks,
    own, cols, panel, inv_parts, first_one, mask_one, mask_rows, own_t, contrib,
    out_a, in_a, marks_out_a, marks_in_a, out_b, marks_b, table,
    recv_sem, mask_recv, send_sem, mask_send, own_sem, cols_sem, out_sem, table_sem,
    send_a, recv_a, marks_send_a, marks_recv_a, send_b, recv_b, marks_send_b, marks_recv_b,
):
    f, g = lax.axis_index("front"), lax.axis_index("grp")
    y, z = lax.rem(g, 4), g // 4
    is_root = g == 0

    barrier = pltpu.get_barrier_semaphore()
    for d in range(1, FRONTS):
        pl.semaphore_signal(barrier, inc=1, device_id={"front": lax.rem(f + d, FRONTS)}, device_id_type=MESH)
    for d in range(1, GROUP):
        pl.semaphore_signal(barrier, inc=1, device_id={"grp": lax.rem(g + d, GROUP)}, device_id_type=MESH)

    def eighth(i):
        return pl.ds(pl.multiple_of(i * 1024, 1024), 1024)

    def tile_rows(r):
        return pl.ds(pl.multiple_of(r * TILE, TILE), TILE)

    @pl.when(is_root)
    def _():
        for i in range(8):
            pltpu.make_async_copy(front.at[0, eighth(i)], cols.at[eighth(i)], cols_sem.at[i]).start()

    for i in range(8):
        pltpu.make_async_copy(front.at[0, eighth(i)], own.at[eighth(i)], own_sem.at[i]).start()

    for c in range(2):
        column = jnp.broadcast_to(mask[0][:, c:c + 1].astype(jnp.float32), (TILES, TILE))
        mask_rows[:, pl.ds(c * TILE, TILE)] = column

        if c == 1:
            @pl.when(is_root)
            def _():
                mask_one[...] = column

    for which in range(2):
        flipped = inverse[0, which].T
        high = flipped.astype(jnp.bfloat16)
        inv_parts[2 * which] = high
        inv_parts[2 * which + 1] = (flipped - high.astype(jnp.float32)).astype(jnp.bfloat16)
    panel[pl.ds(0, TILE), :] = jnp.zeros((TILE, WIDTH), jnp.bfloat16)
    panel[pl.ds(TILE, TILE), pl.ds(TILE, TILE)] = jnp.zeros((TILE, TILE), jnp.bfloat16)

    def mask_part(k):
        return pl.ds(k * 8, 8)

    def rows_of(k, c):
        base = order_row(lax.shift_right_logical(c, SHIFT)) * TILE + k * (TILE // 4) + (c & (SUB - 1)) * CHUNK
        return pl.ds(pl.multiple_of(base, CHUNK), CHUNK)

    def at(turn):
        dy = jnp.where(turn == 0, 1, jnp.where(turn == 2, 3, 0))
        dz = jnp.where(turn == 1, 1, jnp.where(turn == 3, 3, 0))
        return ((z + dz) & 3) * 4 + ((y + dy) & 3)

    places = [tree_place(k, y, z) for k in range(4)]
    counts = [p[1] for p in places]
    children = [[at(turn) for turn in p[2]] for p in places]
    starts = [LAG * p[0] for p in places]
    last_start = jnp.maximum(jnp.maximum(starts[0], starts[1]), jnp.maximum(starts[2], starts[3]))
    last_start = jnp.where(is_root, 0, last_start)

    pl.semaphore_wait(barrier, FRONTS + GROUP - 2)

    @pl.when(is_root)
    def _():
        for k in range(4):
            part = mask_one.at[mask_part(k)]
            send(part, part, mask_send.at[k, 0], mask_recv.at[k], {"grp": children[k][0]})

        def root_send(c, carry):
            for k in range(4):
                rows = rows_of(k, c)
                send(front.at[0, rows], cols.at[rows], send_sem.at[k, 0], recv_sem.at[k, c], {"grp": children[k][0]})
            return carry

        lax.fori_loop(0, STEPS, root_send, 0)
        for i in range(8):
            wait_for(cols.at[eighth(i)], cols_sem.at[i])

    def forward(k, part, sems, recv):
        def child(i):
            @pl.when(counts[k] > i)
            def _():
                send(part, part, sems.at[k, i], recv, {"grp": children[k][i]})
                if i < 2:
                    child(i + 1)

        child(0)

    def make_panel(position):
        r = order_row(position)
        rows = tile_rows(r)
        left = cols[rows, pl.ds(0, TILE)]
        first = (dot_n(left, inv_parts[0]) + dot_n(left, inv_parts[1])).astype(jnp.bfloat16)
        panel[rows, pl.ds(0, TILE)] = first

        @pl.when(position == 0)
        def _():
            first_one[...] = first

        @pl.when(position > 0)
        def _():
            right = cols[rows, pl.ds(TILE, TILE)].astype(jnp.float32)
            right = right - dot_t(first, first_one[...]) * mask_one[pl.ds(r, 1), :]
            high = right.astype(jnp.bfloat16)
            low = (right - high.astype(jnp.float32)).astype(jnp.bfloat16)
            second = dot_n(high, inv_parts[2]) + dot_n(high, inv_parts[3]) + dot_n(low, inv_parts[2])
            panel[rows, pl.ds(TILE, TILE)] = second.astype(jnp.bfloat16)

    def update_tiles(r, product):
        rows = tile_rows(r)
        value = own[rows, :].astype(jnp.float32) - product * mask_rows[pl.ds(r, 1), :]
        lane = lax.broadcasted_iota(jnp.int32, (TILE, WIDTH), 1) // TILE
        value = jnp.where(is_root & (r > lane), panel[rows, :], value.astype(jnp.bfloat16))
        own[rows, :] = value
        return value

    own_position = jnp.where((g == 0) | (g >= 14), ROWS_OUT, TILES - 2 * g)
    own_done = (own_position + 1) * SUB

    def part_a(i):
        return pl.ds(2 * i, 2)

    def contribution_piece(j):
        @pl.when(j == 0)
        def _():
            own_t[...] = panel[pl.ds(pl.multiple_of(g * WIDTH, WIDTH), WIDTH), :].T
            wait_for(own.at[eighth(7)], own_sem.at[7])

        @pl.when((j >= 1) & (j <= ROWS_OUT))
        def _():
            r = TILES - ROWS_OUT - 1 + j
            value = update_tiles(r, dot_n(panel[tile_rows(r), :], own_t[...]))
            contrib[j - 1] = value[:, :TILE]
            contrib[j - 1 + ROWS_OUT] = value[:, TILE:]

        @pl.when((j > ROWS_OUT) & (j <= 2 * ROWS_OUT))
        def _():
            for h in range(2):
                p = 2 * (j - ROWS_OUT - 1) + h
                first, last, label_first, label_last = 0, 0, -1, -1
                for t in reversed(range(SLOTS)):
                    here = lax.shift_right_logical(labels[0, 0, t], 7) == p
                    first = jnp.where(here, t, first)
                    label_first = jnp.where(here, labels[0, 0, t], label_first)
                for t in range(SLOTS):
                    here = lax.shift_right_logical(labels[0, 0, t], 7) == p
                    last = jnp.where(here, t, last)
                    label_last = jnp.where(here, labels[0, 0, t], label_last)
                out_a[2 * p] = contrib[first]
                out_a[2 * p + 1] = contrib[last]
                row = lax.broadcasted_iota(jnp.int32, (8, 128), 0)
                marks_out_a[p] = jnp.where(row == 0, label_first, jnp.where(row == 1, label_last, -1))

        @pl.when((j > ROWS_OUT + 1) & (j <= 2 * ROWS_OUT + 1))
        def _():
            for h in range(2):
                p = 2 * (j - ROWS_OUT - 2) + h
                source, marks = out_a.at[part_a(p)], marks_out_a.at[p]

                @pl.when(p == f)
                def _():
                    pltpu.make_async_copy(source, in_a.at[part_a(f)], recv_a.at[f]).start()
                    pltpu.make_async_copy(marks, marks_in_a.at[f], marks_recv_a.at[f]).start()

                @pl.when(p != f)
                def _():
                    send(marks, marks_in_a.at[f], marks_send_a.at[p], marks_recv_a.at[f], {"front": p})
                    send(source, in_a.at[part_a(f)], send_a.at[p], recv_a.at[f], {"front": p})

    def step(t, carry):
        @pl.when(jnp.logical_not(is_root))
        def _():
            for k in range(4):
                c = t - starts[k]

                @pl.when(c == 0)
                def _():
                    part = mask_one.at[mask_part(k)]
                    wait_for(part, mask_recv.at[k])
                    forward(k, part, mask_send, mask_recv.at[k])

                @pl.when((c >= 0) & (c < STEPS))
                def _():
                    part = cols.at[rows_of(k, c)]
                    wait_for(part, recv_sem.at[k, c])
                    forward(k, part, send_sem, recv_sem.at[k, c])

        done = t + 1 - last_start

        @pl.when((done > 0) & (done <= STEPS) & ((done & (SUB - 1)) == 0))
        def _():
            make_panel(lax.shift_right_logical(done, SHIFT) - 1)

        piece = done - own_done

        @pl.when((piece >= 0) & (piece < PIECES))
        def _():
            contribution_piece(piece)

        return carry

    lax.fori_loop(0, STEPS + LAG * DEPTH + PIECES, step, 0)

    def to_owners():
        for i in range(FRONTS):
            wait_for(marks_in_a.at[i], marks_recv_a.at[i])
        lane = lax.broadcasted_iota(jnp.int32, (1, 128), 1)
        index = jnp.zeros((1, 128), jnp.int32)
        mark = jnp.full((1, 128), -1, jnp.int32)
        for i in range(2 * FRONTS):
            label = marks_in_a[i // 2, pl.ds(i % 2, 1), :]
            here = (label >= 0) & ((lax.shift_right_logical(label, 3) & (GROUP - 1)) == lane)
            index = jnp.where(here, i, index)
            mark = jnp.where(here, label, mark)
        row = lax.broadcasted_iota(jnp.int32, (8, 128), 0)
        marks_b[...] = jnp.where(row == 0, index, mark)
        load = pltpu.make_async_copy(marks_b, table, table_sem)
        load.start()
        load.wait()
        for i in range(FRONTS):
            wait_for(in_a.at[part_a(i)], recv_a.at[i])

        def pack(o, carry):
            out_b[o] = in_a[table[0, o]]
            return carry

        lax.fori_loop(0, GROUP, pack, 0)
        pltpu.make_async_copy(out_b.at[g], arrived.at[g], recv_b.at[g]).start()
        pltpu.make_async_copy(marks_b, arrived_marks.at[g], marks_recv_b.at[g]).start()

        def go(d, carry):
            o = (g + d) & (GROUP - 1)
            send(marks_b, arrived_marks.at[g], marks_send_b.at[o], marks_recv_b.at[g], {"grp": o})
            send(out_b.at[o], arrived.at[g], send_b.at[o], recv_b.at[g], {"grp": o})
            return carry

        lax.fori_loop(1, GROUP, go, 0)

    early = own_position < 20

    @pl.when(early)
    def _():
        to_owners()

    for i in range(7):
        wait_for(own.at[eighth(i)], own_sem.at[i])

    def update(i, carry):
        rows = pl.ds(pl.multiple_of(i * BLOCK, BLOCK), BLOCK)
        product = dot_n(panel[rows, :], own_t[...])
        for h in range(BLOCK // TILE):
            update_tiles(i * (BLOCK // TILE) + h, product[h * TILE:(h + 1) * TILE])
        pltpu.make_async_copy(own.at[rows], out.at[0, rows], out_sem.at[i]).start()
        return carry

    updates = (TILES - ROWS_OUT) * TILE // BLOCK
    lax.fori_loop(0, updates, update, 0)
    bottom = pl.ds((TILES - ROWS_OUT) * TILE, ROWS_OUT * TILE)
    pltpu.make_async_copy(own.at[bottom], out.at[0, bottom], out_sem.at[updates]).start()

    @pl.when(jnp.logical_not(early))
    def _():
        to_owners()

    for k in range(4):
        for i in range(3):
            @pl.when(counts[k] > i)
            def _():
                wait_for(mask_one.at[mask_part(k)], mask_send.at[k, i])
                wait_for(cols.at[pl.ds(0, STEPS * CHUNK)], send_sem.at[k, i])

    def sent_a(d, carry):
        p = (f + d) & (FRONTS - 1)
        wait_for(out_a.at[part_a(p)], send_a.at[p])
        wait_for(marks_out_a.at[p], marks_send_a.at[p])
        return carry

    lax.fori_loop(1, FRONTS, sent_a, 0)

    def sent_b(d, carry):
        o = (g + d) & (GROUP - 1)
        wait_for(out_b.at[o], send_b.at[o])
        wait_for(marks_b, marks_send_b.at[o])
        return carry

    lax.fori_loop(1, GROUP, sent_b, 0)

    def updated(i, carry):
        rows = pl.ds(pl.multiple_of(i * BLOCK, BLOCK), BLOCK)
        wait_for(own.at[rows], out_sem.at[i])
        return carry

    lax.fori_loop(0, updates, updated, 0)
    wait_for(own.at[bottom], out_sem.at[updates])

    def owned(o, carry):
        wait_for(out_b.at[o], recv_b.at[o])
        wait_for(marks_b, marks_recv_b.at[o])
        return carry

    lax.fori_loop(0, GROUP, owned, 0)


def fronts(front, inverse, mask, labels):
    vmem = pl.BlockSpec(memory_space=pltpu.VMEM)
    anywhere = pl.BlockSpec(memory_space=pl.ANY)
    block = pltpu.VMEM((ORDER, WIDTH), jnp.bfloat16)
    tiles = pltpu.VMEM((GROUP, TILE, TILE), jnp.bfloat16)
    dma = pltpu.SemaphoreType.DMA
    return pl.pallas_call(
        fronts_kernel,
        out_shape=(
            jax.ShapeDtypeStruct((1, ORDER, WIDTH), jnp.bfloat16),
            jax.ShapeDtypeStruct((GROUP, TILE, TILE), jnp.bfloat16),
            jax.ShapeDtypeStruct((GROUP, 8, 128), jnp.int32),
        ),
        in_specs=[anywhere, vmem, vmem, pl.BlockSpec(memory_space=pltpu.SMEM)],
        out_specs=(anywhere, anywhere, anywhere),
        scratch_shapes=[
            block, block, block,
            pltpu.VMEM((4, TILE, TILE), jnp.bfloat16),
            pltpu.VMEM((TILE, TILE), jnp.bfloat16),
            pltpu.VMEM((TILES, TILE), jnp.float32),
            pltpu.VMEM((TILES, WIDTH), jnp.float32),
            pltpu.VMEM((WIDTH, WIDTH), jnp.bfloat16),
            pltpu.VMEM((SLOTS, TILE, TILE), jnp.bfloat16),
            tiles, tiles,
            pltpu.VMEM((FRONTS, 8, 128), jnp.int32),
            pltpu.VMEM((FRONTS, 8, 128), jnp.int32),
            tiles,
            pltpu.VMEM((8, 128), jnp.int32),
            pltpu.SMEM((8, 128), jnp.int32),
            dma((4, STEPS)), dma((4,)), dma((4, 3)), dma((4, 3)), dma((8,)), dma((8,)), dma((16,)), dma,
            dma((FRONTS,)), dma((FRONTS,)), dma((FRONTS,)), dma((FRONTS,)),
            dma((GROUP,)), dma((GROUP,)), dma((GROUP,)), dma((GROUP,)),
        ],
        compiler_params=pltpu.CompilerParams(
            collective_id=0, has_side_effects=True, vmem_limit_bytes=64 * 1024 * 1024 - 65536
        ),
        name="fronts",
    )(front, inverse, mask, labels)


def parents_kernel(tiles, marks, out):
    me = lax.axis_index("grp")
    lane = lax.broadcasted_iota(jnp.int32, (1, 128), 1)
    out[...] = jnp.zeros(out.shape, jnp.float32)
    for g in range(GROUP):
        label = jnp.max(jnp.where(lane == me, marks[g, 1:2, :], -1))

        @pl.when(label >= 0)
        def _():
            slot = label & (SLOTS - 1)
            out[slot] += tiles[g].astype(jnp.float32)


def parents(tiles, marks):
    vmem = pl.BlockSpec(memory_space=pltpu.VMEM)
    return pl.pallas_call(
        parents_kernel,
        out_shape=jax.ShapeDtypeStruct((SLOTS, TILE, TILE), jnp.float32),
        in_specs=[vmem, vmem],
        out_specs=vmem,
        name="parents",
    )(tiles, marks)


def shards(front_in, panel_inverse, tile_mask, tile_map):
    result, tiles, marks = fronts(front_in, panel_inverse, tile_mask, tile_map)
    return result, parents(tiles, marks)


def solution(mesh):
    in_specs = (
        P("front", None, "grp"),
        P("front", None, None, None),
        P("front", None, "grp"),
        P("front", "grp", None),
    )
    out_specs = (P("front", None, "grp"), P(("front", "grp"), None, None))
    return jax.shard_map(shards, mesh=mesh, in_specs=in_specs, out_specs=out_specs, check_vma=False)
```

```python
import jax
import jax.numpy as jnp
from jax import lax
from jax.experimental import pallas as pl
from jax.experimental.pallas import tpu as pltpu
from jax.sharding import PartitionSpec as P

TILE = 256
TILES = 32
ORDER = TILE * TILES
WIDTH = 2 * TILE
FRONTS = 8
GROUP = 16
SLOTS = 8
ROWS_OUT = 4
CHUNK = 32
SUB = TILE // (4 * CHUNK)
SHIFT = SUB.bit_length() - 1
STEPS = (TILES - 1) * SUB
LAG = 5
DEPTH = 5
PIECES = 4
BLOCK = 512
PARTS = 4
PART = TILE // PARTS
MESH = pl.DeviceIdType.MESH

TREE_DEPTH = (0, 1, 2, 3, 3, 2, 3, 4, 4, 3, 4, 5, 3, 2, 3, 4)
TREE_SERVES = ((0,), (0, 1, 3), (0, 3), (), (), (0, 1, 2), (0,), (), (), (0, 2), (0,), (), (), (2,), (0,), ())


def entry(table, place):
    words = []
    for half in (table[:8], table[8:]):
        word = sum(value << (4 * i) for i, value in enumerate(half))
        words.append(word - (1 << 32) if word >= 1 << 31 else word)
    word = jnp.where(place < 8, words[0], words[1])
    return lax.shift_right_logical(word, lax.rem(place, 8) * 4) & 15


def tree_place(tree, y, z):
    a = (y, z, lax.rem(4 - y, 4), lax.rem(4 - z, 4))[tree]
    b = (z, lax.rem(4 - y, 4), lax.rem(4 - z, 4), y)[tree]
    place = b * 4 + a
    count = entry([len(v) for v in TREE_SERVES], place)
    turns = [entry([v[i] if len(v) > i else 0 for v in TREE_SERVES], place) for i in range(3)]
    return entry(TREE_DEPTH, place), count, [(turn + tree) & 3 for turn in turns]


def order_row(position):
    return jnp.where(position == 0, 1, jnp.where(position <= ROWS_OUT, 27 + position, TILES - position))


def dot_t(x, y):
    return lax.dot_general(x, y, (((1,), (1,)), ((), ())), preferred_element_type=jnp.float32)


def dot_n(x, y):
    return lax.dot_general(x, y, (((1,), (0,)), ((), ())), preferred_element_type=jnp.float32)


def wait_for(ref, sem):
    pltpu.make_async_copy(ref, ref, sem).wait()


def send(source, target, send_sem, recv_sem, device):
    pltpu.make_async_remote_copy(
        src_ref=source, dst_ref=target, send_sem=send_sem, recv_sem=recv_sem, device_id=device, device_id_type=MESH
    ).start()


def fronts_kernel(
    front, inverse, mask, labels, own, arrived, arrived_marks,
    cols, panel, inv_parts, first_one, mask_one, mask_rows, own_t, contrib,
    out_a, in_a0, in_a1, in_a2, in_a3, marks_out_a, marks_in_a, out_b, marks_b, table,
    recv_sem, mask_recv, send_sem, mask_send, own_sem, cols_sem, table_sem,
    send_a, recv_a, marks_send_a, marks_recv_a, send_b, recv_b, marks_send_b, marks_recv_b,
):
    f, g = lax.axis_index("front"), lax.axis_index("grp")
    y, z = lax.rem(g, 4), g // 4
    is_root = g == 0
    in_a = (in_a0, in_a1, in_a2, in_a3)

    barrier = pltpu.get_barrier_semaphore()
    for d in range(1, FRONTS):
        pl.semaphore_signal(barrier, inc=1, device_id={"front": lax.rem(f + d, FRONTS)}, device_id_type=MESH)
    for d in range(1, GROUP):
        pl.semaphore_signal(barrier, inc=1, device_id={"grp": lax.rem(g + d, GROUP)}, device_id_type=MESH)

    def eighth(i):
        return pl.ds(pl.multiple_of(i * 1024, 1024), 1024)

    def tile_rows(r):
        return pl.ds(pl.multiple_of(r * TILE, TILE), TILE)

    @pl.when(is_root)
    def _():
        for i in range(8):
            pltpu.make_async_copy(front.at[0, eighth(i)], cols.at[eighth(i)], cols_sem.at[i]).start()

    for i in range(8):
        pltpu.make_async_copy(front.at[0, eighth(i)], own.at[eighth(i)], own_sem.at[i]).start()

    for c in range(2):
        column = jnp.broadcast_to(mask[0][:, c:c + 1].astype(jnp.float32), (TILES, TILE))
        mask_rows[:, pl.ds(c * TILE, TILE)] = column

        if c == 1:
            @pl.when(is_root)
            def _():
                mask_one[...] = column

    for which in range(2):
        flipped = inverse[0, which].T
        high = flipped.astype(jnp.bfloat16)
        inv_parts[2 * which] = high
        inv_parts[2 * which + 1] = (flipped - high.astype(jnp.float32)).astype(jnp.bfloat16)
    panel[pl.ds(0, TILE), :] = jnp.zeros((TILE, WIDTH), jnp.bfloat16)
    panel[pl.ds(TILE, TILE), pl.ds(TILE, TILE)] = jnp.zeros((TILE, TILE), jnp.bfloat16)

    def mask_part(k):
        return pl.ds(k * 8, 8)

    def rows_of(k, c):
        base = order_row(lax.shift_right_logical(c, SHIFT)) * TILE + k * (TILE // 4) + (c & (SUB - 1)) * CHUNK
        return pl.ds(pl.multiple_of(base, CHUNK), CHUNK)

    def at(turn):
        dy = jnp.where(turn == 0, 1, jnp.where(turn == 2, 3, 0))
        dz = jnp.where(turn == 1, 1, jnp.where(turn == 3, 3, 0))
        return ((z + dz) & 3) * 4 + ((y + dy) & 3)

    places = [tree_place(k, y, z) for k in range(4)]
    counts = [p[1] for p in places]
    children = [[at(turn) for turn in p[2]] for p in places]
    starts = [LAG * p[0] for p in places]
    last_start = jnp.maximum(jnp.maximum(starts[0], starts[1]), jnp.maximum(starts[2], starts[3]))
    last_start = jnp.where(is_root, 0, last_start)

    pl.semaphore_wait(barrier, FRONTS + GROUP - 2)

    @pl.when(is_root)
    def _():
        for k in range(4):
            part = mask_one.at[mask_part(k)]
            send(part, part, mask_send.at[k, 0], mask_recv.at[k], {"grp": children[k][0]})

        def root_send(c, carry):
            for k in range(4):
                rows = rows_of(k, c)
                send(front.at[0, rows], cols.at[rows], send_sem.at[k, 0], recv_sem.at[k, c], {"grp": children[k][0]})
            return carry

        lax.fori_loop(0, STEPS, root_send, 0)
        for i in range(8):
            wait_for(cols.at[eighth(i)], cols_sem.at[i])

    def forward(k, part, sems, recv):
        def child(i):
            @pl.when(counts[k] > i)
            def _():
                send(part, part, sems.at[k, i], recv, {"grp": children[k][i]})
                if i < 2:
                    child(i + 1)

        child(0)

    def make_panel(position):
        r = order_row(position)
        rows = tile_rows(r)
        left = cols[rows, pl.ds(0, TILE)]
        first = (dot_n(left, inv_parts[0]) + dot_n(left, inv_parts[1])).astype(jnp.bfloat16)
        panel[rows, pl.ds(0, TILE)] = first

        @pl.when(position == 0)
        def _():
            first_one[...] = first

        @pl.when(position > 0)
        def _():
            right = cols[rows, pl.ds(TILE, TILE)].astype(jnp.float32)
            right = right - dot_t(first, first_one[...]) * mask_one[pl.ds(r, 1), :]
            high = right.astype(jnp.bfloat16)
            low = (right - high.astype(jnp.float32)).astype(jnp.bfloat16)
            second = dot_n(high, inv_parts[2]) + dot_n(high, inv_parts[3]) + dot_n(low, inv_parts[2])
            panel[rows, pl.ds(TILE, TILE)] = second.astype(jnp.bfloat16)

    def update_tiles(r, product):
        rows = tile_rows(r)
        value = own[rows, :].astype(jnp.float32) - product * mask_rows[pl.ds(r, 1), :]
        lane = lax.broadcasted_iota(jnp.int32, (TILE, WIDTH), 1) // TILE
        value = jnp.where(is_root & (r > lane), panel[rows, :], value.astype(jnp.bfloat16))
        own[rows, :] = value
        return value

    own_position = jnp.where((g == 0) | (g >= 14), ROWS_OUT, TILES - 2 * g)
    own_done = (own_position + 1) * SUB

    def part_a(i):
        return pl.ds(2 * i, 2)

    def bottom_tiles(r):
        value = update_tiles(r, dot_n(panel[tile_rows(r), :], own_t[...]))
        contrib[r - (TILES - ROWS_OUT)] = value[:, :TILE]
        contrib[r - (TILES - 2 * ROWS_OUT)] = value[:, TILE:]

    def stage_parent(p):
        first, last, label_first, label_last = 0, 0, -1, -1
        for t in reversed(range(SLOTS)):
            here = lax.shift_right_logical(labels[0, 0, t], 7) == p
            first = jnp.where(here, t, first)
            label_first = jnp.where(here, labels[0, 0, t], label_first)
        for t in range(SLOTS):
            here = lax.shift_right_logical(labels[0, 0, t], 7) == p
            last = jnp.where(here, t, last)
            label_last = jnp.where(here, labels[0, 0, t], label_last)
        out_a[2 * p] = contrib[first]
        out_a[2 * p + 1] = contrib[last]
        row = lax.broadcasted_iota(jnp.int32, (8, 128), 0)
        marks_out_a[p] = jnp.where(row == 0, label_first, jnp.where(row == 1, label_last, -1))

    def send_parents():
        pltpu.make_async_copy(marks_out_a.at[f], marks_in_a.at[f], marks_recv_a.at[f]).start()

        def marks_go(d, carry):
            p = (f + d) & (FRONTS - 1)
            send(marks_out_a.at[p], marks_in_a.at[f], marks_send_a.at[p], marks_recv_a.at[f], {"front": p})
            return carry

        lax.fori_loop(1, FRONTS, marks_go, 0)

        for q in range(PARTS):
            rows = pl.ds(q * PART, PART)
            pltpu.make_async_copy(out_a.at[part_a(f), rows], in_a[q].at[part_a(f)], recv_a.at[q, f]).start()

            def go(d, carry):
                p = (f + d) & (FRONTS - 1)
                send(out_a.at[part_a(p), rows], in_a[q].at[part_a(f)], send_a.at[p], recv_a.at[q, f], {"front": p})
                return carry

            lax.fori_loop(1, FRONTS, go, 0)

    def contribution_piece(j):
        @pl.when(j == 0)
        def _():
            own_t[...] = panel[pl.ds(pl.multiple_of(g * WIDTH, WIDTH), WIDTH), :].T
            wait_for(own.at[eighth(7)], own_sem.at[7])

        @pl.when(j <= 1)
        def _():
            bottom_tiles(TILES - ROWS_OUT + 2 * j)
            bottom_tiles(TILES - ROWS_OUT + 2 * j + 1)

        @pl.when(j >= 2)
        def _():
            for h in range(FRONTS // 2):
                stage_parent((j - 2) * (FRONTS // 2) + h)

        @pl.when(j == PIECES - 1)
        def _():
            send_parents()

    def step(t, carry):
        @pl.when(jnp.logical_not(is_root))
        def _():
            for k in range(4):
                c = t - starts[k]

                @pl.when(c == 0)
                def _():
                    part = mask_one.at[mask_part(k)]
                    wait_for(part, mask_recv.at[k])
                    forward(k, part, mask_send, mask_recv.at[k])

                @pl.when((c >= 0) & (c < STEPS))
                def _():
                    part = cols.at[rows_of(k, c)]
                    wait_for(part, recv_sem.at[k, c])
                    forward(k, part, send_sem, recv_sem.at[k, c])

        done = t + 1 - last_start

        @pl.when((done > 0) & (done <= STEPS) & ((done & (SUB - 1)) == 0))
        def _():
            make_panel(lax.shift_right_logical(done, SHIFT) - 1)

        piece = done - own_done

        @pl.when((piece >= 0) & (piece < PIECES))
        def _():
            contribution_piece(piece)

        return carry

    lax.fori_loop(0, STEPS + LAG * DEPTH + PIECES, step, 0)

    def to_owners():
        for i in range(FRONTS):
            wait_for(marks_in_a.at[i], marks_recv_a.at[i])
        lane = lax.broadcasted_iota(jnp.int32, (1, 128), 1)
        index = jnp.zeros((1, 128), jnp.int32)
        mark = jnp.full((1, 128), -1, jnp.int32)
        for i in range(2 * FRONTS):
            label = marks_in_a[i // 2, pl.ds(i % 2, 1), :]
            here = (label >= 0) & ((lax.shift_right_logical(label, 3) & (GROUP - 1)) == lane)
            index = jnp.where(here, i, index)
            mark = jnp.where(here, label, mark)
        row = lax.broadcasted_iota(jnp.int32, (8, 128), 0)
        marks_b[...] = jnp.where(row == 0, index, mark)
        load = pltpu.make_async_copy(marks_b, table, table_sem)
        load.start()
        load.wait()
        pltpu.make_async_copy(marks_b, arrived_marks.at[g], marks_recv_b.at[g]).start()

        def marks_go(d, carry):
            o = (g + d) & (GROUP - 1)
            send(marks_b, arrived_marks.at[g], marks_send_b.at[o], marks_recv_b.at[g], {"grp": o})
            return carry

        lax.fori_loop(1, GROUP, marks_go, 0)

        for q in range(PARTS):
            rows = pl.ds(q * PART, PART)
            for i in range(FRONTS):
                wait_for(in_a[q].at[part_a(i)], recv_a.at[q, i])

            def pack(o, carry):
                out_b[o, rows] = in_a[q][table[0, o]]
                return carry

            lax.fori_loop(0, GROUP, pack, 0)
            pltpu.make_async_copy(out_b.at[g, rows], arrived.at[g, rows], recv_b.at[g]).start()

            def go(d, carry):
                o = (g + d) & (GROUP - 1)
                send(out_b.at[o, rows], arrived.at[g, rows], send_b.at[o], recv_b.at[g], {"grp": o})
                return carry

            lax.fori_loop(1, GROUP, go, 0)

    early = own_position < 20

    @pl.when(early)
    def _():
        to_owners()

    for i in range(7):
        wait_for(own.at[eighth(i)], own_sem.at[i])

    def update(i, carry):
        rows = pl.ds(pl.multiple_of(i * BLOCK, BLOCK), BLOCK)
        product = dot_n(panel[rows, :], own_t[...])
        for h in range(BLOCK // TILE):
            update_tiles(i * (BLOCK // TILE) + h, product[h * TILE:(h + 1) * TILE])
        return carry

    updates = (TILES - ROWS_OUT) * TILE // BLOCK
    lax.fori_loop(0, updates, update, 0)

    @pl.when(jnp.logical_not(early))
    def _():
        to_owners()

    for k in range(4):
        for i in range(3):
            @pl.when(counts[k] > i)
            def _():
                wait_for(mask_one.at[mask_part(k)], mask_send.at[k, i])
                wait_for(cols.at[pl.ds(0, STEPS * CHUNK)], send_sem.at[k, i])

    def sent_a(d, carry):
        p = (f + d) & (FRONTS - 1)
        wait_for(out_a.at[part_a(p)], send_a.at[p])
        wait_for(marks_out_a.at[p], marks_send_a.at[p])
        return carry

    lax.fori_loop(1, FRONTS, sent_a, 0)

    def sent_b(d, carry):
        o = (g + d) & (GROUP - 1)
        wait_for(out_b.at[o], send_b.at[o])
        wait_for(marks_b, marks_send_b.at[o])
        return carry

    lax.fori_loop(1, GROUP, sent_b, 0)

    def owned(o, carry):
        wait_for(out_b.at[o], recv_b.at[o])
        wait_for(marks_b, marks_recv_b.at[o])
        return carry

    lax.fori_loop(0, GROUP, owned, 0)


def fronts(front, inverse, mask, labels):
    vmem = pl.BlockSpec(memory_space=pltpu.VMEM)
    anywhere = pl.BlockSpec(memory_space=pl.ANY)
    block = pltpu.VMEM((ORDER, WIDTH), jnp.bfloat16)
    tiles = pltpu.VMEM((GROUP, TILE, TILE), jnp.bfloat16)
    dma = pltpu.SemaphoreType.DMA
    return pl.pallas_call(
        fronts_kernel,
        out_shape=(
            pltpu.VMEM((ORDER, WIDTH), jnp.bfloat16),
            pltpu.VMEM((GROUP, TILE, TILE), jnp.bfloat16),
            pltpu.VMEM((GROUP, 8, 128), jnp.int32),
        ),
        in_specs=[anywhere, vmem, vmem, pl.BlockSpec(memory_space=pltpu.SMEM)],
        out_specs=(vmem, vmem, vmem),
        scratch_shapes=[
            block, block,
            pltpu.VMEM((4, TILE, TILE), jnp.bfloat16),
            pltpu.VMEM((TILE, TILE), jnp.bfloat16),
            pltpu.VMEM((TILES, TILE), jnp.float32),
            pltpu.VMEM((TILES, WIDTH), jnp.float32),
            pltpu.VMEM((WIDTH, WIDTH), jnp.bfloat16),
            pltpu.VMEM((SLOTS, TILE, TILE), jnp.bfloat16),
            tiles, *[pltpu.VMEM((2 * FRONTS, PART, TILE), jnp.bfloat16)] * PARTS,
            pltpu.VMEM((FRONTS, 8, 128), jnp.int32),
            pltpu.VMEM((FRONTS, 8, 128), jnp.int32),
            tiles,
            pltpu.VMEM((8, 128), jnp.int32),
            pltpu.SMEM((8, 128), jnp.int32),
            dma((4, STEPS)), dma((4,)), dma((4, 3)), dma((4, 3)), dma((8,)), dma((8,)), dma,
            dma((FRONTS,)), dma((PARTS, FRONTS)), dma((FRONTS,)), dma((FRONTS,)),
            dma((GROUP,)), dma((GROUP,)), dma((GROUP,)), dma((GROUP,)),
        ],
        compiler_params=pltpu.CompilerParams(
            collective_id=0, has_side_effects=True, vmem_limit_bytes=44 * 1024 * 1024
        ),
        name="fronts",
    )(front, inverse, mask, labels)


def finish_kernel(own, tiles, marks, front_out, out, sums, front_sem, out_sem):
    me = lax.axis_index("grp")
    lane = lax.broadcasted_iota(jnp.int32, (1, 128), 1)
    keep = [
        pltpu.make_async_copy(own.at[pl.ds(i * 1024, 1024)], front_out.at[0, pl.ds(i * 1024, 1024)], front_sem.at[i])
        for i in range(8)
    ]
    for copy in keep:
        copy.start()
    sums[...] = jnp.zeros(sums.shape, jnp.float32)
    found = [jnp.max(jnp.where(lane == me, marks[g, 1:2, :], -1)) for g in range(GROUP)]
    for g in range(GROUP):
        @pl.when(found[g] >= 0)
        def _():
            slot = found[g] & (SLOTS - 1)
            sums[slot] += tiles[g].astype(jnp.float32)

    save = pltpu.make_async_copy(sums, out, out_sem)
    save.start()
    for copy in keep:
        copy.wait()
    save.wait()


def finish(own, tiles, marks):
    vmem = pl.BlockSpec(memory_space=pltpu.VMEM)
    anywhere = pl.BlockSpec(memory_space=pl.ANY)
    return pl.pallas_call(
        finish_kernel,
        out_shape=(
            jax.ShapeDtypeStruct((1, ORDER, WIDTH), jnp.bfloat16),
            jax.ShapeDtypeStruct((SLOTS, TILE, TILE), jnp.float32),
        ),
        in_specs=[vmem, vmem, vmem],
        out_specs=(anywhere, anywhere),
        scratch_shapes=[
            pltpu.VMEM((SLOTS, TILE, TILE), jnp.float32),
            pltpu.SemaphoreType.DMA((8,)),
            pltpu.SemaphoreType.DMA,
        ],
        compiler_params=pltpu.CompilerParams(vmem_limit_bytes=16 * 1024 * 1024),
        name="finish",
    )(*(pltpu.with_memory_space_constraint(a, pltpu.VMEM) for a in (own, tiles, marks)))


def shards(front_in, panel_inverse, tile_mask, tile_map):
    own, tiles, marks = fronts(front_in, panel_inverse, tile_mask, tile_map)
    return finish(own, tiles, marks)


def solution(mesh):
    in_specs = (
        P("front", None, "grp"),
        P("front", None, None, None),
        P("front", None, "grp"),
        P("front", "grp", None),
    )
    out_specs = (P("front", None, "grp"), P(("front", "grp"), None, None))
    return jax.shard_map(shards, mesh=mesh, in_specs=in_specs, out_specs=out_specs, check_vma=False)
```

```python
import jax
import jax.numpy as jnp
from jax import lax
from jax.experimental import pallas as pl
from jax.experimental.pallas import tpu as pltpu
from jax.sharding import PartitionSpec as P

TILE = 256
TILES = 32
ORDER = TILE * TILES
WIDTH = 2 * TILE
FRONTS = 8
GROUP = 16
SLOTS = 8
ROWS_OUT = 4
CHUNK = 64
SUB = TILE // (4 * CHUNK)
SHIFT = SUB.bit_length() - 1
STEPS = (TILES - 1) * SUB
LAG = 3
DEPTH = 5
PIECES = 4
BLOCK = 512
PARTS = 4
PART = TILE // PARTS
MESH = pl.DeviceIdType.MESH
FRONT_STEPS = (0, 2, 6, 4, 3, 7, 5, 1)
Y_STEPS = (0, 1, 3, 0, 2, 1, 3, 0, 2, 1, 3, 0, 1, 3, 2, 2)
Z_STEPS = (0, 1, 3, 1, 2, 3, 1, 3, 0, 0, 0, 2, 2, 2, 1, 3)

TREE_DEPTH = (0, 1, 2, 3, 3, 2, 3, 4, 4, 3, 4, 5, 3, 2, 3, 4)
TREE_SERVES = ((0,), (0, 1, 3), (0, 3), (), (), (0, 1, 2), (0,), (), (), (0, 2), (0,), (), (), (2,), (0,), ())


def entry(table, place):
    words = []
    for half in (table[:8], table[8:]):
        word = sum(value << (4 * i) for i, value in enumerate(half))
        words.append(word - (1 << 32) if word >= 1 << 31 else word)
    word = jnp.where(place < 8, words[0], words[1])
    return lax.shift_right_logical(word, lax.rem(place, 8) * 4) & 15


def tree_place(tree, y, z):
    a = (y, z, lax.rem(4 - y, 4), lax.rem(4 - z, 4))[tree]
    b = (z, lax.rem(4 - y, 4), lax.rem(4 - z, 4), y)[tree]
    place = b * 4 + a
    count = entry([len(v) for v in TREE_SERVES], place)
    turns = [entry([v[i] if len(v) > i else 0 for v in TREE_SERVES], place) for i in range(3)]
    return entry(TREE_DEPTH, place), count, [(turn + tree) & 3 for turn in turns]


ROW_ORDER = (6, 9, 11, 3, 5, 8, 2, 12, 7, 13, 4, 10, 1)
POSITION = [6 + 2 * ROW_ORDER.index(g) if g in ROW_ORDER else ROWS_OUT for g in range(GROUP)]


def order_row(position):
    later = position - ROWS_OUT - 1
    owner = entry(ROW_ORDER + (0, 0, 0), lax.shift_right_logical(later, 1) & 15)
    row = 2 * owner + 1 - (later & 1)
    return jnp.where(position == 0, 1, jnp.where(position <= ROWS_OUT, 27 + position, row))


def dot_t(x, y):
    return lax.dot_general(x, y, (((1,), (1,)), ((), ())), preferred_element_type=jnp.float32)


def dot_n(x, y):
    return lax.dot_general(x, y, (((1,), (0,)), ((), ())), preferred_element_type=jnp.float32)


def wait_for(ref, sem):
    pltpu.make_async_copy(ref, ref, sem).wait()


def send(source, target, send_sem, recv_sem, device):
    pltpu.make_async_remote_copy(
        src_ref=source, dst_ref=target, send_sem=send_sem, recv_sem=recv_sem, device_id=device, device_id_type=MESH
    ).start()


def fronts_kernel(
    front, inverse, mask, labels, own, arrived, arrived_marks,
    cols, panel, inv_parts, first_one, mask_one, mask_rows, own_t, contrib,
    out_a, in_a0, in_a1, in_a2, in_a3, marks_out_a, marks_in_a, out_b, marks_b, table,
    recv_sem, mask_recv, send_sem, mask_send, own_sem, cols_sem, table_sem,
    send_a, recv_a, marks_send_a, marks_recv_a, send_b, recv_b, marks_send_b, marks_recv_b,
):
    f, g = lax.axis_index("front"), lax.axis_index("grp")
    y, z = lax.rem(g, 4), g // 4
    is_root = g == 0
    in_a = (in_a0, in_a1, in_a2, in_a3)

    barrier = pltpu.get_barrier_semaphore()
    for d in range(1, FRONTS):
        pl.semaphore_signal(barrier, inc=1, device_id={"front": lax.rem(f + d, FRONTS)}, device_id_type=MESH)
    for d in range(1, GROUP):
        pl.semaphore_signal(barrier, inc=1, device_id={"grp": lax.rem(g + d, GROUP)}, device_id_type=MESH)

    def eighth(i):
        return pl.ds(pl.multiple_of(i * 1024, 1024), 1024)

    def tile_rows(r):
        return pl.ds(pl.multiple_of(r * TILE, TILE), TILE)

    @pl.when(is_root)
    def _():
        for i in range(8):
            pltpu.make_async_copy(front.at[0, eighth(i)], cols.at[eighth(i)], cols_sem.at[i]).start()

    for i in range(8):
        pltpu.make_async_copy(front.at[0, eighth(i)], own.at[eighth(i)], own_sem.at[i]).start()

    for c in range(2):
        column = jnp.broadcast_to(mask[0].astype(jnp.float32).T[:, c:c + 1], (TILES, TILE))
        mask_rows[:, pl.ds(c * TILE, TILE)] = column

        if c == 1:
            @pl.when(is_root)
            def _():
                mask_one[...] = column

    for which in range(2):
        flipped = inverse[0, which].T
        high = flipped.astype(jnp.bfloat16)
        inv_parts[2 * which] = high
        inv_parts[2 * which + 1] = (flipped - high.astype(jnp.float32)).astype(jnp.bfloat16)
    panel[pl.ds(0, TILE), :] = jnp.zeros((TILE, WIDTH), jnp.bfloat16)
    panel[pl.ds(TILE, TILE), pl.ds(TILE, TILE)] = jnp.zeros((TILE, TILE), jnp.bfloat16)

    def mask_part(k):
        return pl.ds(k * 8, 8)

    def rows_of(k, c):
        base = order_row(lax.shift_right_logical(c, SHIFT)) * TILE + k * (TILE // 4) + (c & (SUB - 1)) * CHUNK
        return pl.ds(pl.multiple_of(base, CHUNK), CHUNK)

    def at(turn):
        dy = jnp.where(turn == 0, 1, jnp.where(turn == 2, 3, 0))
        dz = jnp.where(turn == 1, 1, jnp.where(turn == 3, 3, 0))
        return ((z + dz) & 3) * 4 + ((y + dy) & 3)

    places = [tree_place(k, y, z) for k in range(4)]
    counts = [p[1] for p in places]
    children = [[at(turn) for turn in p[2]] for p in places]
    starts = [LAG * p[0] for p in places]
    last_start = jnp.maximum(jnp.maximum(starts[0], starts[1]), jnp.maximum(starts[2], starts[3]))
    last_start = jnp.where(is_root, 0, last_start)

    pl.semaphore_wait(barrier, FRONTS + GROUP - 2)

    @pl.when(is_root)
    def _():
        for k in range(4):
            part = mask_one.at[mask_part(k)]
            send(part, part, mask_send.at[k, 0], mask_recv.at[k], {"grp": children[k][0]})

        def root_send(c, carry):
            for k in range(4):
                rows = rows_of(k, c)
                send(front.at[0, rows], cols.at[rows], send_sem.at[k, 0], recv_sem.at[k, c], {"grp": children[k][0]})
            return carry

        lax.fori_loop(0, STEPS, root_send, 0)
        for i in range(8):
            wait_for(cols.at[eighth(i)], cols_sem.at[i])

    def forward(k, part, sems, recv):
        def child(i):
            @pl.when(counts[k] > i)
            def _():
                send(part, part, sems.at[k, i], recv, {"grp": children[k][i]})
                if i < 2:
                    child(i + 1)

        child(0)

    def make_panel(position):
        r = order_row(position)
        rows = tile_rows(r)
        left = cols[rows, pl.ds(0, TILE)]
        first = (dot_n(left, inv_parts[0]) + dot_n(left, inv_parts[1])).astype(jnp.bfloat16)
        panel[rows, pl.ds(0, TILE)] = first

        @pl.when(position == 0)
        def _():
            first_one[...] = first

        @pl.when(position > 0)
        def _():
            right = cols[rows, pl.ds(TILE, TILE)].astype(jnp.float32)
            right = right - dot_t(first, first_one[...]) * mask_one[pl.ds(r, 1), :]
            high = right.astype(jnp.bfloat16)
            low = (right - high.astype(jnp.float32)).astype(jnp.bfloat16)
            second = dot_n(high, inv_parts[2]) + dot_n(high, inv_parts[3]) + dot_n(low, inv_parts[2])
            panel[rows, pl.ds(TILE, TILE)] = second.astype(jnp.bfloat16)

    def update_tiles(r, product):
        rows = tile_rows(r)
        value = own[rows, :].astype(jnp.float32) - product * mask_rows[pl.ds(r, 1), :]
        lane = lax.broadcasted_iota(jnp.int32, (TILE, WIDTH), 1) // TILE
        value = jnp.where(is_root & (r > lane), panel[rows, :], value.astype(jnp.bfloat16))
        own[rows, :] = value
        return value

    own_position = 2 * entry([p // 2 for p in POSITION], g)
    own_done = (own_position + 1) * SUB

    def part_a(i):
        return pl.ds(2 * i, 2)

    def bottom_tiles(r):
        value = update_tiles(r, dot_n(panel[tile_rows(r), :], own_t[...]))
        contrib[r - (TILES - ROWS_OUT)] = value[:, :TILE]
        contrib[r - (TILES - 2 * ROWS_OUT)] = value[:, TILE:]

    def stage_parent(p):
        first, last, label_first, label_last = 0, 0, -1, -1
        for t in reversed(range(SLOTS)):
            here = lax.shift_right_logical(labels[0, 0, t], 7) == p
            first = jnp.where(here, t, first)
            label_first = jnp.where(here, labels[0, 0, t], label_first)
        for t in range(SLOTS):
            here = lax.shift_right_logical(labels[0, 0, t], 7) == p
            last = jnp.where(here, t, last)
            label_last = jnp.where(here, labels[0, 0, t], label_last)
        out_a[2 * p] = contrib[first]
        out_a[2 * p + 1] = contrib[last]
        row = lax.broadcasted_iota(jnp.int32, (8, 128), 0)
        marks_out_a[p] = jnp.where(row == 0, label_first, jnp.where(row == 1, label_last, -1))

    def send_parents():
        pltpu.make_async_copy(marks_out_a.at[f], marks_in_a.at[f], marks_recv_a.at[f]).start()

        def marks_go(d, carry):
            p = (f + d) & (FRONTS - 1)
            send(marks_out_a.at[p], marks_in_a.at[f], marks_send_a.at[p], marks_recv_a.at[f], {"front": p})
            return carry

        lax.fori_loop(1, FRONTS, marks_go, 0)

        for q in range(PARTS):
            rows = pl.ds(q * PART, PART)
            pltpu.make_async_copy(out_a.at[part_a(f), rows], in_a[q].at[part_a(f)], recv_a.at[q, f]).start()

            def go(d, carry):
                p = (f + entry(FRONT_STEPS + FRONT_STEPS, d)) & (FRONTS - 1)
                send(out_a.at[part_a(p), rows], in_a[q].at[part_a(f)], send_a.at[p], recv_a.at[q, f], {"front": p})
                return carry

            lax.fori_loop(1, FRONTS, go, 0)

    def contribution_piece(j):
        @pl.when(j == 0)
        def _():
            own_t[...] = panel[pl.ds(pl.multiple_of(g * WIDTH, WIDTH), WIDTH), :].T
            wait_for(own.at[eighth(7)], own_sem.at[7])

        @pl.when(j <= 1)
        def _():
            bottom_tiles(TILES - ROWS_OUT + 2 * j)
            bottom_tiles(TILES - ROWS_OUT + 2 * j + 1)

        @pl.when(j >= 2)
        def _():
            for h in range(FRONTS // 2):
                stage_parent((j - 2) * (FRONTS // 2) + h)

        @pl.when(j == PIECES - 1)
        def _():
            send_parents()

    def step(t, carry):
        @pl.when(jnp.logical_not(is_root))
        def _():
            for k in range(4):
                c = t - starts[k]

                @pl.when(c == 0)
                def _():
                    part = mask_one.at[mask_part(k)]
                    wait_for(part, mask_recv.at[k])
                    forward(k, part, mask_send, mask_recv.at[k])

                @pl.when((c >= 0) & (c < STEPS))
                def _():
                    part = cols.at[rows_of(k, c)]
                    wait_for(part, recv_sem.at[k, c])
                    forward(k, part, send_sem, recv_sem.at[k, c])

        done = t + 1 - last_start

        @pl.when((done > 0) & (done <= STEPS) & ((done & (SUB - 1)) == 0))
        def _():
            make_panel(lax.shift_right_logical(done, SHIFT) - 1)

        piece = done - own_done

        @pl.when((piece >= 0) & (piece < PIECES))
        def _():
            contribution_piece(piece)

        return carry

    lax.fori_loop(0, STEPS + LAG * DEPTH + PIECES, step, 0)

    def to_owners():
        for i in range(FRONTS):
            wait_for(marks_in_a.at[i], marks_recv_a.at[i])
        lane = lax.broadcasted_iota(jnp.int32, (1, 128), 1)
        index = jnp.zeros((1, 128), jnp.int32)
        mark = jnp.full((1, 128), -1, jnp.int32)
        for i in range(2 * FRONTS):
            label = marks_in_a[i // 2, pl.ds(i % 2, 1), :]
            here = (label >= 0) & ((lax.shift_right_logical(label, 3) & (GROUP - 1)) == lane)
            index = jnp.where(here, i, index)
            mark = jnp.where(here, label, mark)
        row = lax.broadcasted_iota(jnp.int32, (8, 128), 0)
        marks_b[...] = jnp.where(row == 0, index, mark)
        load = pltpu.make_async_copy(marks_b, table, table_sem)
        load.start()
        load.wait()
        pltpu.make_async_copy(marks_b, arrived_marks.at[g], marks_recv_b.at[g]).start()

        def marks_go(d, carry):
            o = (g + d) & (GROUP - 1)
            send(marks_b, arrived_marks.at[g], marks_send_b.at[o], marks_recv_b.at[g], {"grp": o})
            return carry

        lax.fori_loop(1, GROUP, marks_go, 0)

        for q in range(PARTS):
            rows = pl.ds(q * PART, PART)
            for i in range(FRONTS):
                wait_for(in_a[q].at[part_a(i)], recv_a.at[q, i])

            def pack(o, carry):
                out_b[o, rows] = in_a[q][table[0, o]]
                return carry

            lax.fori_loop(0, GROUP, pack, 0)
            pltpu.make_async_copy(out_b.at[g, rows], arrived.at[g, rows], recv_b.at[g]).start()

            def go(d, carry):
                o = ((z + entry(Z_STEPS, d)) & 3) * 4 + ((y + entry(Y_STEPS, d)) & 3)
                send(out_b.at[o, rows], arrived.at[g, rows], send_b.at[o], recv_b.at[g], {"grp": o})
                return carry

            lax.fori_loop(1, GROUP, go, 0)

    early = own_position < 20

    @pl.when(early)
    def _():
        to_owners()

    for i in range(7):
        wait_for(own.at[eighth(i)], own_sem.at[i])

    def update(i, carry):
        rows = pl.ds(pl.multiple_of(i * BLOCK, BLOCK), BLOCK)
        product = dot_n(panel[rows, :], own_t[...])
        for h in range(BLOCK // TILE):
            update_tiles(i * (BLOCK // TILE) + h, product[h * TILE:(h + 1) * TILE])
        return carry

    updates = (TILES - ROWS_OUT) * TILE // BLOCK
    lax.fori_loop(0, updates, update, 0)

    @pl.when(jnp.logical_not(early))
    def _():
        to_owners()

    for k in range(4):
        for i in range(3):
            @pl.when(counts[k] > i)
            def _():
                wait_for(mask_one.at[mask_part(k)], mask_send.at[k, i])
                wait_for(cols.at[pl.ds(0, STEPS * CHUNK)], send_sem.at[k, i])

    def sent_a(d, carry):
        p = (f + d) & (FRONTS - 1)
        wait_for(out_a.at[part_a(p)], send_a.at[p])
        wait_for(marks_out_a.at[p], marks_send_a.at[p])
        return carry

    lax.fori_loop(1, FRONTS, sent_a, 0)

    def sent_b(d, carry):
        o = (g + d) & (GROUP - 1)
        wait_for(out_b.at[o], send_b.at[o])
        wait_for(marks_b, marks_send_b.at[o])
        return carry

    lax.fori_loop(1, GROUP, sent_b, 0)

    def owned(o, carry):
        wait_for(out_b.at[o], recv_b.at[o])
        wait_for(marks_b, marks_recv_b.at[o])
        return carry

    lax.fori_loop(0, GROUP, owned, 0)


def fronts(front, inverse, mask, labels):
    vmem = pl.BlockSpec(memory_space=pltpu.VMEM)
    anywhere = pl.BlockSpec(memory_space=pl.ANY)
    block = pltpu.VMEM((ORDER, WIDTH), jnp.bfloat16)
    tiles = pltpu.VMEM((GROUP, TILE, TILE), jnp.bfloat16)
    dma = pltpu.SemaphoreType.DMA
    return pl.pallas_call(
        fronts_kernel,
        out_shape=(
            pltpu.VMEM((ORDER, WIDTH), jnp.bfloat16),
            pltpu.VMEM((GROUP, TILE, TILE), jnp.bfloat16),
            pltpu.VMEM((GROUP, 8, 128), jnp.int32),
        ),
        in_specs=[anywhere, vmem, vmem, pl.BlockSpec(memory_space=pltpu.SMEM)],
        out_specs=(vmem, vmem, vmem),
        scratch_shapes=[
            block, block,
            pltpu.VMEM((4, TILE, TILE), jnp.bfloat16),
            pltpu.VMEM((TILE, TILE), jnp.bfloat16),
            pltpu.VMEM((TILES, TILE), jnp.float32),
            pltpu.VMEM((TILES, WIDTH), jnp.float32),
            pltpu.VMEM((WIDTH, WIDTH), jnp.bfloat16),
            pltpu.VMEM((SLOTS, TILE, TILE), jnp.bfloat16),
            tiles, *[pltpu.VMEM((2 * FRONTS, PART, TILE), jnp.bfloat16)] * PARTS,
            pltpu.VMEM((FRONTS, 8, 128), jnp.int32),
            pltpu.VMEM((FRONTS, 8, 128), jnp.int32),
            tiles,
            pltpu.VMEM((8, 128), jnp.int32),
            pltpu.SMEM((8, 128), jnp.int32),
            dma((4, STEPS)), dma((4,)), dma((4, 3)), dma((4, 3)), dma((8,)), dma((8,)), dma,
            dma((FRONTS,)), dma((PARTS, FRONTS)), dma((FRONTS,)), dma((FRONTS,)),
            dma((GROUP,)), dma((GROUP,)), dma((GROUP,)), dma((GROUP,)),
        ],
        compiler_params=pltpu.CompilerParams(
            collective_id=0, has_side_effects=True, vmem_limit_bytes=44 * 1024 * 1024
        ),
        name="fronts",
    )(front, inverse, mask, labels)


def finish_kernel(own, tiles, marks, front_out, out, sums, front_sem, out_sem):
    me = lax.axis_index("grp")
    lane = lax.broadcasted_iota(jnp.int32, (1, 128), 1)
    keep = [
        pltpu.make_async_copy(own.at[pl.ds(i * 1024, 1024)], front_out.at[0, pl.ds(i * 1024, 1024)], front_sem.at[i])
        for i in range(8)
    ]
    for copy in keep:
        copy.start()
    sums[...] = jnp.zeros(sums.shape, jnp.float32)
    found = [jnp.max(jnp.where(lane == me, marks[g, 1:2, :], -1)) for g in range(GROUP)]
    for g in range(GROUP):
        @pl.when(found[g] >= 0)
        def _():
            slot = found[g] & (SLOTS - 1)
            sums[slot] += tiles[g].astype(jnp.float32)

    save = pltpu.make_async_copy(sums, out, out_sem)
    save.start()
    for copy in keep:
        copy.wait()
    save.wait()


def finish(own, tiles, marks):
    vmem = pl.BlockSpec(memory_space=pltpu.VMEM)
    anywhere = pl.BlockSpec(memory_space=pl.ANY)
    return pl.pallas_call(
        finish_kernel,
        out_shape=(
            jax.ShapeDtypeStruct((1, ORDER, WIDTH), jnp.bfloat16),
            jax.ShapeDtypeStruct((SLOTS, TILE, TILE), jnp.float32),
        ),
        in_specs=[vmem, vmem, vmem],
        out_specs=(anywhere, anywhere),
        scratch_shapes=[
            pltpu.VMEM((SLOTS, TILE, TILE), jnp.float32),
            pltpu.SemaphoreType.DMA((8,)),
            pltpu.SemaphoreType.DMA,
        ],
        compiler_params=pltpu.CompilerParams(vmem_limit_bytes=16 * 1024 * 1024),
        name="finish",
    )(*(pltpu.with_memory_space_constraint(a, pltpu.VMEM) for a in (own, tiles, marks)))


def shards(front_in, panel_inverse, tile_mask, tile_map):
    own, tiles, marks = fronts(front_in, panel_inverse, jnp.swapaxes(tile_mask, 1, 2), tile_map)
    return finish(own, tiles, marks)


def solution(mesh):
    in_specs = (
        P("front", None, "grp"),
        P("front", None, None, None),
        P("front", None, "grp"),
        P("front", "grp", None),
    )
    out_specs = (P("front", None, "grp"), P(("front", "grp"), None, None))
    return jax.shard_map(shards, mesh=mesh, in_specs=in_specs, out_specs=out_specs, check_vma=False)
```

```python
import jax
import jax.numpy as jnp
from jax import lax
from jax.experimental import pallas as pl
from jax.experimental.pallas import tpu as pltpu
from jax.sharding import PartitionSpec as P

TILE = 256
TILES = 32
ORDER = TILE * TILES
WIDTH = 2 * TILE
FRONTS = 8
GROUP = 16
SLOTS = 8
ROWS_OUT = 4
CHUNK = TILE // 4
STEPS = TILES - 1
LAG = 3

PIECES = 2
BLOCK = 512
PARTS = 2
PART = TILE // PARTS
MESH = pl.DeviceIdType.MESH
FRONT_STEPS = (0, 2, 6, 4, 3, 7, 5, 1)
Y_STEPS = (0, 1, 3, 0, 2, 1, 3, 0, 2, 1, 3, 0, 1, 3, 2, 2)
Z_STEPS = (0, 1, 3, 1, 2, 3, 1, 3, 0, 0, 0, 2, 2, 2, 1, 3)

TREE_DEPTH = (0, 1, 2, 3, 3, 2, 3, 4, 4, 3, 4, 5, 3, 2, 3, 4)
TREE_SERVES = ((0,), (0, 1, 3), (0, 3), (), (), (0, 1, 2), (0,), (), (), (0, 2), (0,), (), (), (2,), (0,), ())

def entry(table, place):
    words = []
    for half in (table[:8], table[8:]):
        word = sum(value << (4 * i) for i, value in enumerate(half))
        words.append(word - (1 << 32) if word >= 1 << 31 else word)
    word = jnp.where(place < 8, words[0], words[1])
    return lax.shift_right_logical(word, lax.rem(place, 8) * 4) & 15

def tree_place(tree, y, z):
    a = (y, z, lax.rem(4 - y, 4), lax.rem(4 - z, 4))[tree]
    b = (z, lax.rem(4 - y, 4), lax.rem(4 - z, 4), y)[tree]
    place = b * 4 + a
    count = entry([len(v) for v in TREE_SERVES], place)
    turns = [entry([v[i] if len(v) > i else 0 for v in TREE_SERVES], place) for i in range(3)]
    return entry(TREE_DEPTH, place), count, [(turn + tree) & 3 for turn in turns]

ROW_ORDER = (6, 9, 11, 5, 8, 2, 7, 13, 10)
NEIGHBOURS = (1, 4, 3, 12)
SHARED = 1 + ROWS_OUT + 2 * len(ROW_ORDER)
POSITION = [6 + 2 * ROW_ORDER.index(g) if g in ROW_ORDER else ROWS_OUT for g in range(GROUP)]

def order_row(position):
    later = position - ROWS_OUT - 1
    owner = entry(ROW_ORDER + (0,) * 7, lax.shift_right_logical(later, 1) & 15)
    row = 2 * owner + 1 - (later & 1)
    return jnp.where(position == 0, 1, jnp.where(position <= ROWS_OUT, 27 + position, row))

def dot_t(x, y):
    return lax.dot_general(x, y, (((1,), (1,)), ((), ())), preferred_element_type=jnp.float32)

def dot_n(x, y):
    return lax.dot_general(x, y, (((1,), (0,)), ((), ())), preferred_element_type=jnp.float32)

def wait_for(ref, sem):
    pltpu.make_async_copy(ref, ref, sem).wait()

def send(source, target, send_sem, recv_sem, device):
    pltpu.make_async_remote_copy(
        src_ref=source, dst_ref=target, send_sem=send_sem, recv_sem=recv_sem, device_id=device, device_id_type=MESH
    ).start()

def fronts_kernel(
    front, inverse, mask, labels, own, arrived, arrived_marks,
    cols, panel, inv_parts, first_one, mask_one, mask_rows, own_t, contrib,
    out_a, in_a0, in_a1, marks_out_a, marks_in_a, out_b, marks_b, table,
    recv_sem, mask_recv, send_sem, mask_send, own_sem, cols_sem, table_sem,
    send_a, recv_a, marks_send_a, marks_recv_a, send_b, recv_b, marks_send_b, marks_recv_b,
):
    f, g = lax.axis_index("front"), lax.axis_index("grp")
    y, z = lax.rem(g, 4), g // 4
    is_root = g == 0
    in_a = (in_a0, in_a1)

    barrier = pltpu.get_barrier_semaphore()
    for d in range(1, FRONTS):
        pl.semaphore_signal(barrier, inc=1, device_id={"front": lax.rem(f + d, FRONTS)}, device_id_type=MESH)
    for d in range(1, GROUP):
        pl.semaphore_signal(barrier, inc=1, device_id={"grp": lax.rem(g + d, GROUP)}, device_id_type=MESH)

    def eighth(i):
        return pl.ds(pl.multiple_of(i * 1024, 1024), 1024)

    def tile_rows(r):
        return pl.ds(pl.multiple_of(r * TILE, TILE), TILE)

    @pl.when(is_root)
    def _():
        for i in range(8):
            pltpu.make_async_copy(front.at[0, eighth(i)], cols.at[eighth(i)], cols_sem.at[i]).start()

    for i in range(8):
        pltpu.make_async_copy(front.at[0, eighth(i)], own.at[eighth(i)], own_sem.at[i]).start()

    for c in range(2):
        column = jnp.broadcast_to(mask[0].astype(jnp.float32).T[:, c:c + 1], (TILES, TILE))
        mask_rows[:, pl.ds(c * TILE, TILE)] = column

        if c == 1:
            @pl.when(is_root)
            def _():
                mask_one[...] = column

    for which in range(2):
        flipped = inverse[0, which].T
        high = flipped.astype(jnp.bfloat16)
        inv_parts[2 * which] = high
        inv_parts[2 * which + 1] = (flipped - high.astype(jnp.float32)).astype(jnp.bfloat16)
    panel[pl.ds(0, TILE), :] = jnp.zeros((TILE, WIDTH), jnp.bfloat16)
    panel[pl.ds(TILE, TILE), pl.ds(TILE, TILE)] = jnp.zeros((TILE, TILE), jnp.bfloat16)

    def mask_part(k):
        return pl.ds(k * 8, 8)

    def rows_of(k, c):
        shared = order_row(c) * TILE + k * CHUNK
        base = jnp.where(c < SHARED, shared, 2 * NEIGHBOURS[k] * TILE + (c - SHARED) * CHUNK)
        return pl.ds(pl.multiple_of(base, CHUNK), CHUNK)

    def at(turn):
        dy = jnp.where(turn == 0, 1, jnp.where(turn == 2, 3, 0))
        dz = jnp.where(turn == 1, 1, jnp.where(turn == 3, 3, 0))
        return ((z + dz) & 3) * 4 + ((y + dy) & 3)

    places = [tree_place(k, y, z) for k in range(4)]
    counts = [p[1] for p in places]
    children = [[at(turn) for turn in p[2]] for p in places]
    starts = [LAG * p[0] for p in places]
    last_start = jnp.maximum(jnp.maximum(starts[0], starts[1]), jnp.maximum(starts[2], starts[3]))
    last_start = jnp.where(is_root, 0, last_start)

    pl.semaphore_wait(barrier, FRONTS + GROUP - 2)

    @pl.when(is_root)
    def _():
        for k in range(4):
            part = mask_one.at[mask_part(k)]
            send(part, part, mask_send.at[k, 0], mask_recv.at[k], {"grp": children[k][0]})

        def root_send(c, carry):
            for k in range(4):
                rows = rows_of(k, c)
                send(front.at[0, rows], cols.at[rows], send_sem.at[k, 0], recv_sem.at[k, c], {"grp": children[k][0]})
            return carry

        lax.fori_loop(0, STEPS, root_send, 0)
        for i in range(8):
            wait_for(cols.at[eighth(i)], cols_sem.at[i])

    def forward(k, part, sems, recv):
        def child(i):
            @pl.when(counts[k] > i)
            def _():
                send(part, part, sems.at[k, i], recv, {"grp": children[k][i]})
                if i < 2:
                    child(i + 1)

        child(0)

    def make_panel(r):
        rows = tile_rows(r)
        left = cols[rows, pl.ds(0, TILE)]
        first = (dot_n(left, inv_parts[0]) + dot_n(left, inv_parts[1])).astype(jnp.bfloat16)
        panel[rows, pl.ds(0, TILE)] = first

        @pl.when(r == 1)
        def _():
            first_one[...] = first

        @pl.when(r > 1)
        def _():
            right = cols[rows, pl.ds(TILE, TILE)].astype(jnp.float32)
            right = right - dot_t(first, first_one[...]) * mask_one[pl.ds(r, 1), :]
            high = right.astype(jnp.bfloat16)
            low = (right - high.astype(jnp.float32)).astype(jnp.bfloat16)
            second = dot_n(high, inv_parts[2]) + dot_n(high, inv_parts[3]) + dot_n(low, inv_parts[2])
            panel[rows, pl.ds(TILE, TILE)] = second.astype(jnp.bfloat16)

    def update_tiles(r, product):
        rows = tile_rows(r)
        value = own[rows, :].astype(jnp.float32) - product * mask_rows[pl.ds(r, 1), :]
        lane = lax.broadcasted_iota(jnp.int32, (TILE, WIDTH), 1) // TILE
        value = jnp.where(is_root & (r > lane), panel[rows, :], value.astype(jnp.bfloat16))
        own[rows, :] = value
        return value

    own_position = 2 * entry([p // 2 for p in POSITION], g)
    beside_root = entry([int(v in NEIGHBOURS) for v in range(GROUP)], g) == 1
    own_step = jnp.where(beside_root, STEPS - 1 + LAG, own_position + last_start)

    def part_a(i):
        return pl.ds(2 * i, 2)

    def bottom_tiles(r):
        value = update_tiles(r, dot_n(panel[tile_rows(r), :], own_t[...]))
        contrib[r - (TILES - ROWS_OUT)] = value[:, :TILE]
        contrib[r - (TILES - 2 * ROWS_OUT)] = value[:, TILE:]

    def stage_parent(p):
        first, last, label_first, label_last = 0, 0, -1, -1
        for t in reversed(range(SLOTS)):
            here = lax.shift_right_logical(labels[0, 0, t], 7) == p
            first = jnp.where(here, t, first)
            label_first = jnp.where(here, labels[0, 0, t], label_first)
        for t in range(SLOTS):
            here = lax.shift_right_logical(labels[0, 0, t], 7) == p
            last = jnp.where(here, t, last)
            label_last = jnp.where(here, labels[0, 0, t], label_last)
        out_a[2 * p] = contrib[first]
        out_a[2 * p + 1] = contrib[last]
        row = lax.broadcasted_iota(jnp.int32, (8, 128), 0)
        marks_out_a[p] = jnp.where(row == 0, label_first, jnp.where(row == 1, label_last, -1))

    def send_parents():
        pltpu.make_async_copy(marks_out_a.at[f], marks_in_a.at[f], marks_recv_a.at[f]).start()

        def marks_go(d, carry):
            p = (f + d) & (FRONTS - 1)
            send(marks_out_a.at[p], marks_in_a.at[f], marks_send_a.at[p], marks_recv_a.at[f], {"front": p})
            return carry

        lax.fori_loop(1, FRONTS, marks_go, 0)

        for q in range(PARTS):
            rows = pl.ds(q * PART, PART)
            pltpu.make_async_copy(out_a.at[part_a(f), rows], in_a[q].at[part_a(f)], recv_a.at[q, f]).start()

            def go(d, carry):
                p = (f + entry(FRONT_STEPS + FRONT_STEPS, d)) & (FRONTS - 1)
                send(out_a.at[part_a(p), rows], in_a[q].at[part_a(f)], send_a.at[p], recv_a.at[q, f], {"front": p})
                return carry

            lax.fori_loop(1, FRONTS, go, 0)

    def contribution_piece(j):
        @pl.when(j == 0)
        def _():
            own_t[...] = panel[pl.ds(pl.multiple_of(g * WIDTH, WIDTH), WIDTH), :].T
            wait_for(own.at[eighth(7)], own_sem.at[7])
            for r in range(TILES - ROWS_OUT, TILES):
                bottom_tiles(r)

        @pl.when(j == PIECES - 1)
        def _():
            for p in range(FRONTS):
                stage_parent(p)
            send_parents()

    def step(t, carry):
        @pl.when(jnp.logical_not(is_root))
        def _():
            for k in range(4):
                c = t - starts[k]

                @pl.when(c == 0)
                def _():
                    part = mask_one.at[mask_part(k)]
                    wait_for(part, mask_recv.at[k])
                    forward(k, part, mask_send, mask_recv.at[k])

                @pl.when((c >= 0) & (c < STEPS))
                def _():
                    part = cols.at[rows_of(k, c)]
                    wait_for(part, recv_sem.at[k, c])
                    forward(k, part, send_sem, recv_sem.at[k, c])

        position = t - last_start

        @pl.when((position >= 0) & (position < SHARED))
        def _():
            make_panel(order_row(position))

        for k in range(4):
            c = t - starts[k]

            @pl.when((c == SHARED + 3) | (c == SHARED + 7))
            def _():
                make_panel(2 * NEIGHBOURS[k] + (c == SHARED + 7).astype(jnp.int32))

        piece = t - own_step

        @pl.when((piece >= 0) & (piece < PIECES))
        def _():
            contribution_piece(piece)

        return carry

    lax.fori_loop(0, jnp.maximum(last_start + STEPS, own_step + PIECES + 1), step, 0)

    def to_owners():
        for i in range(FRONTS):
            wait_for(marks_in_a.at[i], marks_recv_a.at[i])
        lane = lax.broadcasted_iota(jnp.int32, (1, 128), 1)
        index = jnp.zeros((1, 128), jnp.int32)
        mark = jnp.full((1, 128), -1, jnp.int32)
        for i in range(2 * FRONTS):
            label = marks_in_a[i // 2, pl.ds(i % 2, 1), :]
            here = (label >= 0) & ((lax.shift_right_logical(label, 3) & (GROUP - 1)) == lane)
            index = jnp.where(here, i, index)
            mark = jnp.where(here, label, mark)
        row = lax.broadcasted_iota(jnp.int32, (8, 128), 0)
        marks_b[...] = jnp.where(row == 0, index, mark)
        load = pltpu.make_async_copy(marks_b, table, table_sem)
        load.start()
        load.wait()
        pltpu.make_async_copy(marks_b, arrived_marks.at[g], marks_recv_b.at[g]).start()

        def marks_go(d, carry):
            o = (g + d) & (GROUP - 1)
            send(marks_b, arrived_marks.at[g], marks_send_b.at[o], marks_recv_b.at[g], {"grp": o})
            return carry

        lax.fori_loop(1, GROUP, marks_go, 0)

        for q in range(PARTS):
            rows = pl.ds(q * PART, PART)
            for i in range(FRONTS):
                wait_for(in_a[q].at[part_a(i)], recv_a.at[q, i])

            def pack(o, carry):
                out_b[o, rows] = in_a[q][table[0, o]]
                return carry

            lax.fori_loop(0, GROUP, pack, 0)
            pltpu.make_async_copy(out_b.at[g, rows], arrived.at[g, rows], recv_b.at[g]).start()

            def go(d, carry):
                o = ((z + entry(Z_STEPS, d)) & 3) * 4 + ((y + entry(Y_STEPS, d)) & 3)
                send(out_b.at[o, rows], arrived.at[g, rows], send_b.at[o], recv_b.at[g], {"grp": o})
                return carry

            lax.fori_loop(1, GROUP, go, 0)

    early = (own_position < 20) & jnp.logical_not(beside_root)

    @pl.when(early)
    def _():
        to_owners()

    for i in range(7):
        wait_for(own.at[eighth(i)], own_sem.at[i])

    def update(i, carry):
        rows = pl.ds(pl.multiple_of(i * BLOCK, BLOCK), BLOCK)
        product = dot_n(panel[rows, :], own_t[...])
        for h in range(BLOCK // TILE):
            update_tiles(i * (BLOCK // TILE) + h, product[h * TILE:(h + 1) * TILE])
        return carry

    updates = (TILES - ROWS_OUT) * TILE // BLOCK
    lax.fori_loop(0, updates, update, 0)

    @pl.when(jnp.logical_not(early))
    def _():
        to_owners()

    for k in range(4):
        for i in range(3):
            @pl.when(counts[k] > i)
            def _():
                wait_for(mask_one.at[mask_part(k)], mask_send.at[k, i])
                wait_for(cols.at[pl.ds(0, STEPS * CHUNK)], send_sem.at[k, i])

    def sent_a(d, carry):
        p = (f + d) & (FRONTS - 1)
        wait_for(out_a.at[part_a(p)], send_a.at[p])
        wait_for(marks_out_a.at[p], marks_send_a.at[p])
        return carry

    lax.fori_loop(1, FRONTS, sent_a, 0)

    def sent_b(d, carry):
        o = (g + d) & (GROUP - 1)
        wait_for(out_b.at[o], send_b.at[o])
        wait_for(marks_b, marks_send_b.at[o])
        return carry

    lax.fori_loop(1, GROUP, sent_b, 0)

    def owned(o, carry):
        wait_for(out_b.at[o], recv_b.at[o])
        wait_for(marks_b, marks_recv_b.at[o])
        return carry

    lax.fori_loop(0, GROUP, owned, 0)

def fronts(front, inverse, mask, labels):
    vmem = pl.BlockSpec(memory_space=pltpu.VMEM)
    anywhere = pl.BlockSpec(memory_space=pl.ANY)
    block = pltpu.VMEM((ORDER, WIDTH), jnp.bfloat16)
    tiles = pltpu.VMEM((GROUP, TILE, TILE), jnp.bfloat16)
    dma = pltpu.SemaphoreType.DMA
    return pl.pallas_call(
        fronts_kernel,
        out_shape=(
            pltpu.VMEM((ORDER, WIDTH), jnp.bfloat16),
            pltpu.VMEM((GROUP, TILE, TILE), jnp.bfloat16),
            pltpu.VMEM((GROUP, 8, 128), jnp.int32),
        ),
        in_specs=[anywhere, vmem, vmem, pl.BlockSpec(memory_space=pltpu.SMEM)],
        out_specs=(vmem, vmem, vmem),
        scratch_shapes=[
            block, block,
            pltpu.VMEM((4, TILE, TILE), jnp.bfloat16),
            pltpu.VMEM((TILE, TILE), jnp.bfloat16),
            pltpu.VMEM((TILES, TILE), jnp.float32),
            pltpu.VMEM((TILES, WIDTH), jnp.float32),
            pltpu.VMEM((WIDTH, WIDTH), jnp.bfloat16),
            pltpu.VMEM((SLOTS, TILE, TILE), jnp.bfloat16),
            tiles, *[pltpu.VMEM((2 * FRONTS, PART, TILE), jnp.bfloat16)] * PARTS,
            pltpu.VMEM((FRONTS, 8, 128), jnp.int32),
            pltpu.VMEM((FRONTS, 8, 128), jnp.int32),
            tiles,
            pltpu.VMEM((8, 128), jnp.int32),
            pltpu.SMEM((8, 128), jnp.int32),
            dma((4, STEPS)), dma((4,)), dma((4, 3)), dma((4, 3)), dma((8,)), dma((8,)), dma,
            dma((FRONTS,)), dma((PARTS, FRONTS)), dma((FRONTS,)), dma((FRONTS,)),
            dma((GROUP,)), dma((GROUP,)), dma((GROUP,)), dma((GROUP,)),
        ],
        compiler_params=pltpu.CompilerParams(
            collective_id=0, has_side_effects=True, vmem_limit_bytes=44 * 1024 * 1024
        ),
        name="fronts",
    )(front, inverse, mask, labels)

def finish_kernel(own, tiles, marks, front_out, out, sums, front_sem, out_sem):
    me = lax.axis_index("grp")
    lane = lax.broadcasted_iota(jnp.int32, (1, 128), 1)
    keep = [
        pltpu.make_async_copy(own.at[pl.ds(i * 1024, 1024)], front_out.at[0, pl.ds(i * 1024, 1024)], front_sem.at[i])
        for i in range(8)
    ]
    for copy in keep:
        copy.start()
    sums[...] = jnp.zeros(sums.shape, jnp.float32)
    found = [jnp.max(jnp.where(lane == me, marks[g, 1:2, :], -1)) for g in range(GROUP)]
    for g in range(GROUP):
        @pl.when(found[g] >= 0)
        def _():
            slot = found[g] & (SLOTS - 1)
            sums[slot] += tiles[g].astype(jnp.float32)

    save = pltpu.make_async_copy(sums, out, out_sem)
    save.start()
    for copy in keep:
        copy.wait()
    save.wait()

def finish(own, tiles, marks):
    vmem = pl.BlockSpec(memory_space=pltpu.VMEM)
    anywhere = pl.BlockSpec(memory_space=pl.ANY)
    return pl.pallas_call(
        finish_kernel,
        out_shape=(
            jax.ShapeDtypeStruct((1, ORDER, WIDTH), jnp.bfloat16),
            jax.ShapeDtypeStruct((SLOTS, TILE, TILE), jnp.float32),
        ),
        in_specs=[vmem, vmem, vmem],
        out_specs=(anywhere, anywhere),
        scratch_shapes=[
            pltpu.VMEM((SLOTS, TILE, TILE), jnp.float32),
            pltpu.SemaphoreType.DMA((8,)),
            pltpu.SemaphoreType.DMA,
        ],
        compiler_params=pltpu.CompilerParams(vmem_limit_bytes=16 * 1024 * 1024),
        name="finish",
    )(*(pltpu.with_memory_space_constraint(a, pltpu.VMEM) for a in (own, tiles, marks)))

def shards(front_in, panel_inverse, tile_mask, tile_map):
    own, tiles, marks = fronts(front_in, panel_inverse, jnp.swapaxes(tile_mask, 1, 2), tile_map)
    return finish(own, tiles, marks)

def solution(mesh):
    in_specs = (
        P("front", None, "grp"),
        P("front", None, None, None),
        P("front", None, "grp"),
        P("front", "grp", None),
    )
    out_specs = (P("front", None, "grp"), P(("front", "grp"), None, None))
    return jax.shard_map(shards, mesh=mesh, in_specs=in_specs, out_specs=out_specs, check_vma=False)
```

```python
import jax
import jax.numpy as jnp
from jax import lax
from jax.experimental import pallas as pl
from jax.experimental.pallas import tpu as pltpu
from jax.sharding import PartitionSpec as P

TILE = 256
TILES = 32
ORDER = TILE * TILES
WIDTH = 2 * TILE
FRONTS = 8
GROUP = 16
SLOTS = 8
ROWS_OUT = 4
CHUNK = TILE // 4
STEPS = TILES - 1
LAG = 3

PIECES = 2
BLOCK = 512
PARTS = 2
PART = TILE // PARTS
MESH = pl.DeviceIdType.MESH
FRONT_STEPS = (0, 4, 2, 6, 5, 3, 7, 1)
Y_STEPS = (0, 1, 3, 0, 2, 1, 3, 0, 2, 1, 3, 0, 1, 3, 2, 2)
Z_STEPS = (0, 1, 3, 1, 2, 3, 1, 3, 0, 0, 0, 2, 2, 2, 1, 3)

TREE_DEPTH = (0, 1, 2, 3, 3, 2, 3, 4, 4, 3, 4, 5, 3, 2, 3, 4)
TREE_SERVES = ((0,), (0, 1, 3), (0, 3), (), (), (0, 1, 2), (0,), (), (), (0, 2), (0,), (), (), (2,), (0,), ())

def entry(table, place):
    words = []
    for half in (table[:8], table[8:]):
        word = sum(value << (4 * i) for i, value in enumerate(half))
        words.append(word - (1 << 32) if word >= 1 << 31 else word)
    word = jnp.where(place < 8, words[0], words[1])
    return lax.shift_right_logical(word, lax.rem(place, 8) * 4) & 15

def tree_place(tree, y, z):
    a = (y, z, lax.rem(4 - y, 4), lax.rem(4 - z, 4))[tree]
    b = (z, lax.rem(4 - y, 4), lax.rem(4 - z, 4), y)[tree]
    place = b * 4 + a
    count = entry([len(v) for v in TREE_SERVES], place)
    turns = [entry([v[i] if len(v) > i else 0 for v in TREE_SERVES], place) for i in range(3)]
    return entry(TREE_DEPTH, place), count, [(turn + tree) & 3 for turn in turns]

ROW_ORDER = (6, 9, 11, 5, 8, 2, 7, 13, 10)
NEIGHBOURS = (1, 4, 3, 12)
SHARED = 1 + ROWS_OUT + 2 * len(ROW_ORDER)
POSITION = [6 + 2 * ROW_ORDER.index(g) if g in ROW_ORDER else ROWS_OUT for g in range(GROUP)]

def order_row(position):
    later = position - ROWS_OUT - 1
    owner = entry(ROW_ORDER + (0,) * 7, lax.shift_right_logical(later, 1) & 15)
    row = 2 * owner + 1 - (later & 1)
    return jnp.where(position == 0, 1, jnp.where(position <= ROWS_OUT, 27 + position, row))

def dot_t(x, y):
    return lax.dot_general(x, y, (((1,), (1,)), ((), ())), preferred_element_type=jnp.float32)

def dot_n(x, y):
    return lax.dot_general(x, y, (((1,), (0,)), ((), ())), preferred_element_type=jnp.float32)

def wait_for(ref, sem):
    pltpu.make_async_copy(ref, ref, sem).wait()

def send(source, target, send_sem, recv_sem, device):
    pltpu.make_async_remote_copy(
        src_ref=source, dst_ref=target, send_sem=send_sem, recv_sem=recv_sem, device_id=device, device_id_type=MESH
    ).start()

def fronts_kernel(
    front, inverse, mask, labels, own, arrived, arrived_marks,
    cols, panel, inv_parts, first_one, mask_one, mask_rows, own_t, contrib,
    out_a, in_a0, in_a1, marks_out_a, marks_in_a, out_b, marks_b, table,
    recv_sem, mask_recv, send_sem, mask_send, own_sem, cols_sem, table_sem,
    send_a, recv_a, marks_send_a, marks_recv_a, send_b, recv_b, marks_send_b, marks_recv_b,
):
    f, g = lax.axis_index("front"), lax.axis_index("grp")
    y, z = lax.rem(g, 4), g // 4
    is_root = g == 0
    in_a = (in_a0, in_a1)

    barrier = pltpu.get_barrier_semaphore()
    for d in range(1, FRONTS):
        pl.semaphore_signal(barrier, inc=1, device_id={"front": lax.rem(f + d, FRONTS)}, device_id_type=MESH)
    for d in range(1, GROUP):
        pl.semaphore_signal(barrier, inc=1, device_id={"grp": lax.rem(g + d, GROUP)}, device_id_type=MESH)

    def eighth(i):
        return pl.ds(pl.multiple_of(i * 1024, 1024), 1024)

    def tile_rows(r):
        return pl.ds(pl.multiple_of(r * TILE, TILE), TILE)

    @pl.when(is_root)
    def _():
        for i in range(8):
            pltpu.make_async_copy(front.at[0, eighth(i)], cols.at[eighth(i)], cols_sem.at[i]).start()

    for i in range(8):
        pltpu.make_async_copy(front.at[0, eighth(i)], own.at[eighth(i)], own_sem.at[i]).start()

    for c in range(2):
        column = jnp.broadcast_to(mask[0].astype(jnp.float32).T[:, c:c + 1], (TILES, TILE))
        mask_rows[:, pl.ds(c * TILE, TILE)] = column

        if c == 1:
            @pl.when(is_root)
            def _():
                mask_one[...] = column

    for which in range(2):
        flipped = inverse[0, which].T
        high = flipped.astype(jnp.bfloat16)
        inv_parts[2 * which] = high
        inv_parts[2 * which + 1] = (flipped - high.astype(jnp.float32)).astype(jnp.bfloat16)
    panel[pl.ds(0, TILE), :] = jnp.zeros((TILE, WIDTH), jnp.bfloat16)
    panel[pl.ds(TILE, TILE), pl.ds(TILE, TILE)] = jnp.zeros((TILE, TILE), jnp.bfloat16)

    def mask_part(k):
        return pl.ds(k * 8, 8)

    def rows_of(k, c):
        shared = order_row(c) * TILE + k * CHUNK
        base = jnp.where(c < SHARED, shared, 2 * NEIGHBOURS[k] * TILE + (c - SHARED) * CHUNK)
        return pl.ds(pl.multiple_of(base, CHUNK), CHUNK)

    def at(turn):
        dy = jnp.where(turn == 0, 1, jnp.where(turn == 2, 3, 0))
        dz = jnp.where(turn == 1, 1, jnp.where(turn == 3, 3, 0))
        return ((z + dz) & 3) * 4 + ((y + dy) & 3)

    places = [tree_place(k, y, z) for k in range(4)]
    counts = [p[1] for p in places]
    children = [[at(turn) for turn in p[2]] for p in places]
    starts = [LAG * p[0] for p in places]
    last_start = jnp.maximum(jnp.maximum(starts[0], starts[1]), jnp.maximum(starts[2], starts[3]))
    last_start = jnp.where(is_root, 0, last_start)

    pl.semaphore_wait(barrier, FRONTS + GROUP - 2)

    @pl.when(is_root)
    def _():
        for k in range(4):
            part = mask_one.at[mask_part(k)]
            send(part, part, mask_send.at[k, 0], mask_recv.at[k], {"grp": children[k][0]})

        def root_send(c, carry):
            for k in range(4):
                rows = rows_of(k, c)
                send(front.at[0, rows], cols.at[rows], send_sem.at[k, 0], recv_sem.at[k, c], {"grp": children[k][0]})
            return carry

        lax.fori_loop(0, STEPS, root_send, 0)
        for i in range(8):
            wait_for(cols.at[eighth(i)], cols_sem.at[i])

    def forward(k, part, sems, recv):
        def child(i):
            @pl.when(counts[k] > i)
            def _():
                send(part, part, sems.at[k, i], recv, {"grp": children[k][i]})
                if i < 2:
                    child(i + 1)

        child(0)

    def make_panel(r):
        rows = tile_rows(r)
        left = cols[rows, pl.ds(0, TILE)]
        first = (dot_n(left, inv_parts[0]) + dot_n(left, inv_parts[1])).astype(jnp.bfloat16)
        panel[rows, pl.ds(0, TILE)] = first

        @pl.when(r == 1)
        def _():
            first_one[...] = first

        @pl.when(r > 1)
        def _():
            right = cols[rows, pl.ds(TILE, TILE)].astype(jnp.float32)
            right = right - dot_t(first, first_one[...]) * mask_one[pl.ds(r, 1), :]
            high = right.astype(jnp.bfloat16)
            low = (right - high.astype(jnp.float32)).astype(jnp.bfloat16)
            second = dot_n(high, inv_parts[2]) + dot_n(high, inv_parts[3]) + dot_n(low, inv_parts[2])
            panel[rows, pl.ds(TILE, TILE)] = second.astype(jnp.bfloat16)

    def update_tiles(r, product):
        rows = tile_rows(r)
        value = own[rows, :].astype(jnp.float32) - product * mask_rows[pl.ds(r, 1), :]
        lane = lax.broadcasted_iota(jnp.int32, (TILE, WIDTH), 1) // TILE
        value = jnp.where(is_root & (r > lane), panel[rows, :], value.astype(jnp.bfloat16))
        own[rows, :] = value
        return value

    own_position = 2 * entry([p // 2 for p in POSITION], g)
    beside_root = entry([int(v in NEIGHBOURS) for v in range(GROUP)], g) == 1
    own_step = jnp.where(beside_root, STEPS - 1 + LAG, own_position + last_start)

    def part_a(i):
        return pl.ds(2 * i, 2)

    def bottom_tiles(r):
        value = update_tiles(r, dot_n(panel[tile_rows(r), :], own_t[...]))
        contrib[r - (TILES - ROWS_OUT)] = value[:, :TILE]
        contrib[r - (TILES - 2 * ROWS_OUT)] = value[:, TILE:]

    def stage_parent(p):
        first, last, label_first, label_last = 0, 0, -1, -1
        for t in reversed(range(SLOTS)):
            here = lax.shift_right_logical(labels[0, 0, t], 7) == p
            first = jnp.where(here, t, first)
            label_first = jnp.where(here, labels[0, 0, t], label_first)
        for t in range(SLOTS):
            here = lax.shift_right_logical(labels[0, 0, t], 7) == p
            last = jnp.where(here, t, last)
            label_last = jnp.where(here, labels[0, 0, t], label_last)
        out_a[2 * p] = contrib[first]
        out_a[2 * p + 1] = contrib[last]
        row = lax.broadcasted_iota(jnp.int32, (8, 128), 0)
        marks_out_a[p] = jnp.where(row == 0, label_first, jnp.where(row == 1, label_last, -1))

    def send_parents():
        pltpu.make_async_copy(marks_out_a.at[f], marks_in_a.at[f], marks_recv_a.at[f]).start()

        def marks_go(d, carry):
            p = (f + d) & (FRONTS - 1)
            send(marks_out_a.at[p], marks_in_a.at[f], marks_send_a.at[p], marks_recv_a.at[f], {"front": p})
            return carry

        lax.fori_loop(1, FRONTS, marks_go, 0)

        for q in range(PARTS):
            rows = pl.ds(q * PART, PART)
            pltpu.make_async_copy(out_a.at[part_a(f), rows], in_a[q].at[part_a(f)], recv_a.at[q, f]).start()

            def go(d, carry):
                p = (f + entry(FRONT_STEPS + FRONT_STEPS, d)) & (FRONTS - 1)
                send(out_a.at[part_a(p), rows], in_a[q].at[part_a(f)], send_a.at[p], recv_a.at[q, f], {"front": p})
                return carry

            lax.fori_loop(1, FRONTS, go, 0)

    def contribution_piece(j):
        @pl.when(j == 0)
        def _():
            own_t[...] = panel[pl.ds(pl.multiple_of(g * WIDTH, WIDTH), WIDTH), :].T
            wait_for(own.at[eighth(7)], own_sem.at[7])
            for r in range(TILES - ROWS_OUT, TILES):
                bottom_tiles(r)

        @pl.when(j == PIECES - 1)
        def _():
            for p in range(FRONTS):
                stage_parent(p)
            send_parents()

    def step(t, carry):
        @pl.when(jnp.logical_not(is_root))
        def _():
            for k in range(4):
                c = t - starts[k]

                @pl.when(c == 0)
                def _():
                    part = mask_one.at[mask_part(k)]
                    wait_for(part, mask_recv.at[k])
                    forward(k, part, mask_send, mask_recv.at[k])

                @pl.when((c >= 0) & (c < STEPS))
                def _():
                    part = cols.at[rows_of(k, c)]
                    wait_for(part, recv_sem.at[k, c])
                    forward(k, part, send_sem, recv_sem.at[k, c])

        position = t - last_start

        @pl.when((position >= 0) & (position < SHARED))
        def _():
            make_panel(order_row(position))

        for k in range(4):
            c = t - starts[k]

            @pl.when((c == SHARED + 3) | (c == SHARED + 7))
            def _():
                make_panel(2 * NEIGHBOURS[k] + (c == SHARED + 7).astype(jnp.int32))

        piece = t - own_step

        @pl.when((piece >= 0) & (piece < PIECES))
        def _():
            contribution_piece(piece)

        return carry

    lax.fori_loop(0, jnp.maximum(last_start + STEPS, own_step + PIECES + 1), step, 0)

    def to_owners():
        for i in range(FRONTS):
            wait_for(marks_in_a.at[i], marks_recv_a.at[i])
        lane = lax.broadcasted_iota(jnp.int32, (1, 128), 1)
        index = jnp.zeros((1, 128), jnp.int32)
        mark = jnp.full((1, 128), -1, jnp.int32)
        for i in range(2 * FRONTS):
            label = marks_in_a[i // 2, pl.ds(i % 2, 1), :]
            here = (label >= 0) & ((lax.shift_right_logical(label, 3) & (GROUP - 1)) == lane)
            index = jnp.where(here, i, index)
            mark = jnp.where(here, label, mark)
        row = lax.broadcasted_iota(jnp.int32, (8, 128), 0)
        marks_b[...] = jnp.where(row == 0, index, mark)
        load = pltpu.make_async_copy(marks_b, table, table_sem)
        load.start()
        load.wait()
        pltpu.make_async_copy(marks_b, arrived_marks.at[g], marks_recv_b.at[g]).start()

        def marks_go(d, carry):
            o = (g + d) & (GROUP - 1)
            send(marks_b, arrived_marks.at[g], marks_send_b.at[o], marks_recv_b.at[g], {"grp": o})
            return carry

        lax.fori_loop(1, GROUP, marks_go, 0)

        for q in range(PARTS):
            rows = pl.ds(q * PART, PART)
            for i in range(FRONTS):
                wait_for(in_a[q].at[part_a(i)], recv_a.at[q, i])

            def pack(o, carry):
                out_b[o, rows] = in_a[q][table[0, o]]
                return carry

            lax.fori_loop(0, GROUP, pack, 0)
            pltpu.make_async_copy(out_b.at[g, rows], arrived.at[g, rows], recv_b.at[g]).start()

            def go(d, carry):
                o = ((z + entry(Z_STEPS, d)) & 3) * 4 + ((y + entry(Y_STEPS, d)) & 3)
                send(out_b.at[o, rows], arrived.at[g, rows], send_b.at[o], recv_b.at[g], {"grp": o})
                return carry

            lax.fori_loop(1, GROUP, go, 0)

    early = (own_position < 20) & jnp.logical_not(beside_root)

    @pl.when(early)
    def _():
        to_owners()

    for i in range(7):
        wait_for(own.at[eighth(i)], own_sem.at[i])

    def update(i, carry):
        rows = pl.ds(pl.multiple_of(i * BLOCK, BLOCK), BLOCK)
        product = dot_n(panel[rows, :], own_t[...])
        for h in range(BLOCK // TILE):
            update_tiles(i * (BLOCK // TILE) + h, product[h * TILE:(h + 1) * TILE])
        return carry

    updates = (TILES - ROWS_OUT) * TILE // BLOCK
    lax.fori_loop(0, updates, update, 0)

    @pl.when(jnp.logical_not(early))
    def _():
        to_owners()

    for k in range(4):
        for i in range(3):
            @pl.when(counts[k] > i)
            def _():
                wait_for(mask_one.at[mask_part(k)], mask_send.at[k, i])
                wait_for(cols.at[pl.ds(0, STEPS * CHUNK)], send_sem.at[k, i])

    def sent_a(d, carry):
        p = (f + d) & (FRONTS - 1)
        wait_for(out_a.at[part_a(p)], send_a.at[p])
        wait_for(marks_out_a.at[p], marks_send_a.at[p])
        return carry

    lax.fori_loop(1, FRONTS, sent_a, 0)

    def sent_b(d, carry):
        o = (g + d) & (GROUP - 1)
        wait_for(out_b.at[o], send_b.at[o])
        wait_for(marks_b, marks_send_b.at[o])
        return carry

    lax.fori_loop(1, GROUP, sent_b, 0)

    def owned(o, carry):
        wait_for(out_b.at[o], recv_b.at[o])
        wait_for(marks_b, marks_recv_b.at[o])
        return carry

    lax.fori_loop(0, GROUP, owned, 0)

def fronts(front, inverse, mask, labels):
    vmem = pl.BlockSpec(memory_space=pltpu.VMEM)
    anywhere = pl.BlockSpec(memory_space=pl.ANY)
    block = pltpu.VMEM((ORDER, WIDTH), jnp.bfloat16)
    tiles = pltpu.VMEM((GROUP, TILE, TILE), jnp.bfloat16)
    dma = pltpu.SemaphoreType.DMA
    return pl.pallas_call(
        fronts_kernel,
        out_shape=(
            pltpu.VMEM((ORDER, WIDTH), jnp.bfloat16),
            pltpu.VMEM((GROUP, TILE, TILE), jnp.bfloat16),
            pltpu.VMEM((GROUP, 8, 128), jnp.int32),
        ),
        in_specs=[anywhere, vmem, vmem, pl.BlockSpec(memory_space=pltpu.SMEM)],
        out_specs=(vmem, vmem, vmem),
        scratch_shapes=[
            block, block,
            pltpu.VMEM((4, TILE, TILE), jnp.bfloat16),
            pltpu.VMEM((TILE, TILE), jnp.bfloat16),
            pltpu.VMEM((TILES, TILE), jnp.float32),
            pltpu.VMEM((TILES, WIDTH), jnp.float32),
            pltpu.VMEM((WIDTH, WIDTH), jnp.bfloat16),
            pltpu.VMEM((SLOTS, TILE, TILE), jnp.bfloat16),
            tiles, *[pltpu.VMEM((2 * FRONTS, PART, TILE), jnp.bfloat16)] * PARTS,
            pltpu.VMEM((FRONTS, 8, 128), jnp.int32),
            pltpu.VMEM((FRONTS, 8, 128), jnp.int32),
            tiles,
            pltpu.VMEM((8, 128), jnp.int32),
            pltpu.SMEM((8, 128), jnp.int32),
            dma((4, STEPS)), dma((4,)), dma((4, 3)), dma((4, 3)), dma((8,)), dma((8,)), dma,
            dma((FRONTS,)), dma((PARTS, FRONTS)), dma((FRONTS,)), dma((FRONTS,)),
            dma((GROUP,)), dma((GROUP,)), dma((GROUP,)), dma((GROUP,)),
        ],
        compiler_params=pltpu.CompilerParams(
            collective_id=0, has_side_effects=True, vmem_limit_bytes=44 * 1024 * 1024
        ),
        name="fronts",
    )(front, inverse, mask, labels)

def finish_kernel(own, tiles, marks, front_out, out, sums, front_sem, out_sem):
    me = lax.axis_index("grp")
    lane = lax.broadcasted_iota(jnp.int32, (1, 128), 1)
    keep = [
        pltpu.make_async_copy(own.at[pl.ds(i * 1024, 1024)], front_out.at[0, pl.ds(i * 1024, 1024)], front_sem.at[i])
        for i in range(8)
    ]
    for copy in keep:
        copy.start()
    sums[...] = jnp.zeros(sums.shape, jnp.float32)
    found = [jnp.max(jnp.where(lane == me, marks[g, 1:2, :], -1)) for g in range(GROUP)]
    for g in range(GROUP):
        @pl.when(found[g] >= 0)
        def _():
            slot = found[g] & (SLOTS - 1)
            sums[slot] += tiles[g].astype(jnp.float32)

    save = pltpu.make_async_copy(sums, out, out_sem)
    save.start()
    for copy in keep:
        copy.wait()
    save.wait()

def finish(own, tiles, marks):
    vmem = pl.BlockSpec(memory_space=pltpu.VMEM)
    anywhere = pl.BlockSpec(memory_space=pl.ANY)
    return pl.pallas_call(
        finish_kernel,
        out_shape=(
            jax.ShapeDtypeStruct((1, ORDER, WIDTH), jnp.bfloat16),
            jax.ShapeDtypeStruct((SLOTS, TILE, TILE), jnp.float32),
        ),
        in_specs=[vmem, vmem, vmem],
        out_specs=(anywhere, anywhere),
        scratch_shapes=[
            pltpu.VMEM((SLOTS, TILE, TILE), jnp.float32),
            pltpu.SemaphoreType.DMA((8,)),
            pltpu.SemaphoreType.DMA,
        ],
        compiler_params=pltpu.CompilerParams(vmem_limit_bytes=16 * 1024 * 1024),
        name="finish",
    )(*(pltpu.with_memory_space_constraint(a, pltpu.VMEM) for a in (own, tiles, marks)))

def shards(front_in, panel_inverse, tile_mask, tile_map):
    own, tiles, marks = fronts(front_in, panel_inverse, jnp.swapaxes(tile_mask, 1, 2), tile_map)
    return finish(own, tiles, marks)

def solution(mesh):
    in_specs = (
        P("front", None, "grp"),
        P("front", None, None, None),
        P("front", None, "grp"),
        P("front", "grp", None),
    )
    out_specs = (P("front", None, "grp"), P(("front", "grp"), None, None))
    return jax.shard_map(shards, mesh=mesh, in_specs=in_specs, out_specs=out_specs, check_vma=False)
```
